128 devices in a mesh: expert: 64 (over z, y, x), fsdp: 2 (over core).
Axes of the slice: x: 4, y: 4, z: 4, core: 2. Of those that a mesh axis runs over, the one named last changes fastest.
Arguments:
- out_grad: bfloat16 [8192, 2560], P('expert', 'fsdp'), may hold values from -6 to 6
- expert_ids: int32 [8192, 6], P('expert'), may hold values from 0 to 63, all different within a row; in each aligned block of 128 rows (0 to 127, 128 to 255, ...) at most 18 rows name the same one
- gate_probs: float32 [8192, 6], P('expert'), may hold values from 0.02 to 0.6
- saved_inputs: bfloat16 [64, 1152, 2560], P('expert', 'fsdp'), may hold values from -6 to 6
- gate_weight: bfloat16 [64, 2560, 768], P('expert', 'fsdp'), may hold values from -0.125 to 0.125
- up_weight: bfloat16 [64, 2560, 768], P('expert', 'fsdp'), may hold values from -0.125 to 0.125
- down_weight: bfloat16 [64, 2560, 768], P('expert', 'fsdp'), may hold values from -0.21875 to 0.21875
Outputs:
- input_grad: bfloat16 [8192, 2560], P('expert', 'fsdp')
- gate_grad: bfloat16 [8192, 6], P('expert')
- down_grad: float32 [64, 2560, 768], P('expert', 'fsdp')
The draws below stay inside these ranges and needn't reach their ends.
Inputs may be any that keep to these rules, and one draw needn't show every extreme that they name: `expert_ids`: each row names 6 different experts. The rows of one block of 128 tokens name any one expert at most 18 times, and in every draw the rows of some block name some expert exactly 18 times.
All inputs are finite; a program needn't handle non-finite values.
Results may differ from the reference program's by a relative error of at most 0.011.
Values may be sent and summed in bfloat16 or wider, within the bound.
A program may use at most 128 MiB of HBM per device.

```python
import math
import jax
import jax.numpy as jnp
import numpy as np
from jax import lax

D = 2560
H = 768
TOPK = 6
TOK_DEV = 128
EXPERTS = 64
CAP = 18
SLOTS = 1152
TOKENS = 8192


def level_of(rng, extent, shards, least, largest):
    loudness, own = 1.0, jax.random.fold_in(rng, 6)
    for position, shards_of in shards:
        steps = jnp.exp(jax.random.uniform(jax.random.fold_in(own, position), (shards_of,), jnp.float32, least / len(shards), largest / len(shards)))
        loudness = loudness * jnp.repeat(steps, extent[position] // shards_of).reshape([-1 if axis == position else 1 for axis in range(len(extent))])
    return loudness


def routed_block(own_key, own, number, rows, amount, top, reach, skew):
    ranking = jax.random.permutation(own_key, amount)
    heavy_load, usual = load_shares(amount, rows * top, reach, skew, True), load_shares(amount, rows * top, reach, skew, False)
    places = jnp.arange(amount)

    def named(tallies, rotation):
        used = int((tallies > 0).sum())
        fixed = max(1, used // 4)
        shifted = fixed + (places - fixed + rotation * (used - fixed)) % max(1, amount - fixed)
        return jnp.zeros((amount,), jnp.int32).at[ranking[jnp.where(places < fixed, places, shifted)]].set(jnp.asarray(tallies, jnp.int32))

    tallies = jnp.where(number % 4 == 0, named(heavy_load, number // 4), named(usual, number - number // 4 - 1))
    mixed = jax.random.permutation(jax.random.fold_in(own, 3), amount)
    donor, sink = mixed[0:amount // 2 * 2:2], mixed[1:amount // 2 * 2:2]
    margin = jnp.minimum(tallies[donor] - 1, reach - tallies[sink]) // 2
    margin = jnp.where((donor == ranking[0]) | (sink == ranking[0]) | (tallies[sink] == 0), 0, jnp.maximum(margin, 0))
    shifted = jax.random.randint(jax.random.fold_in(own, 4), (amount // 2,), 0, 1 << 20) % (margin + 1)
    tallies = tallies.at[donor].add(-shifted).at[sink].add(shifted)
    members = jnp.searchsorted(jnp.cumsum(tallies), jnp.arange(rows * top), side="right").astype(jnp.int32)
    table = members.reshape(top, rows).T
    table = table[jax.random.permutation(jax.random.fold_in(own, 1), rows)]
    rotation = jax.random.randint(jax.random.fold_in(own, 2), (rows, 1), 0, top)
    return jnp.take_along_axis(table, (jnp.arange(top)[None, :] + rotation) % top, axis=1)


def load_shares(count, total, bound, lean, full):
    loads = [(1 << 20) // math.isqrt(standing ** lean) + 1 for standing in range(1, count + 1)]
    largest = bound if full else min(bound, max(-(-total // count), total * loads[0] // sum(loads)))
    least = 1 if total - largest >= count - 1 else 0
    holding, rest = [largest] + [least] * (count - 1), total - largest - least * (count - 1)
    while rest > 0:
        candidates = [i for i in range(1, count) if holding[i] < largest] or [i for i in range(1, count) if holding[i] < bound]
        mass, left = sum([loads[i] for i in candidates]), rest
        for i in candidates:
            extra = min(bound - holding[i], max(1, left * loads[i] // mass), rest)
            holding[i] = holding[i] + extra
            rest = rest - extra
    return np.array(holding)


def bell_draw(rng, extent, scale, most, shards=(), kind=jnp.bfloat16):
    array = scale * jax.random.normal(rng, extent, jnp.float32)
    if shards:
        array = array * level_of(rng, extent, shards, -0.22, 0.18)
    return jnp.clip(array, -most, most).astype(kind)


def setup_inputs(seed: int = 0) -> dict:
    keys = jax.random.split(jax.random.key(seed), 8)
    out_grad = bell_draw(keys[0], (TOKENS, D), 1.0, 6.0, ((0, 64), (1, 2)))
    expert_ids_keys = jax.random.split(jax.random.fold_in(keys[1], 1), TOKENS // TOK_DEV)
    expert_ids_turns = jax.random.permutation(jax.random.fold_in(keys[1], 3), TOKENS // TOK_DEV)
    expert_ids = jax.vmap(lambda own, number: routed_block(jax.random.fold_in(keys[1], 2), own, number, TOK_DEV, EXPERTS, TOPK, CAP, 2))(expert_ids_keys, expert_ids_turns).reshape((TOKENS, TOPK))
    gate_probs = jnp.clip(jnp.exp(math.log(0.6) - 3.4011974 * jax.random.uniform(keys[2], (TOKENS, TOPK), jnp.float32) ** level_of(keys[2], (TOKENS, TOPK), ((0, 64),), -0.2, 0.2)), 0.02, 0.6)
    saved_inputs = bell_draw(keys[3], (EXPERTS, SLOTS, D), 1.0, 6.0, ((0, 64), (1, 2)))
    gate_weight = bell_draw(keys[4], (EXPERTS, D, H), D ** -0.5, 0.125, ((0, 64), (1, 2)))
    up_weight = bell_draw(keys[5], (EXPERTS, D, H), D ** -0.5, 0.125, ((0, 64), (1, 2)))
    down_weight = bell_draw(keys[6], (EXPERTS, D, H), H ** -0.5, 0.21875, ((0, 64), (1, 2)))
    return {"out_grad": out_grad, "expert_ids": expert_ids, "gate_probs": gate_probs, "saved_inputs": saved_inputs, "gate_weight": gate_weight, "up_weight": up_weight, "down_weight": down_weight}


def reference(out_grad, expert_ids, gate_probs, saved_inputs, gate_weight, up_weight, down_weight):
    token_count, model_width = out_grad.shape
    top_count = expert_ids.shape[1]
    expert_count = gate_weight.shape[0]
    slot_count = saved_inputs.shape[1]
    route_count = token_count * top_count
    block_count = token_count // TOK_DEV
    block_ids = expert_ids.reshape(block_count, TOK_DEV * top_count)
    route_table = (block_ids[:, :, None] == jnp.arange(expert_count, dtype=jnp.int32)[None, None, :]).astype(jnp.int32)
    earlier = jnp.cumsum(route_table, axis=1) - route_table
    route_rank = jnp.sum(earlier * route_table, axis=2).astype(jnp.int32)
    block_index = jnp.arange(block_count, dtype=jnp.int32)
    route_row = (block_index[:, None] * CAP + route_rank).reshape(route_count).astype(jnp.int32)
    flat_ids = expert_ids.reshape(route_count)
    route_index = jnp.arange(route_count, dtype=jnp.int32)
    token_of_route = route_index // top_count
    probs_half = gate_probs.reshape(route_count).astype(jnp.bfloat16)

    def one_expert(carried, expert_index):
        input_sum, gate_slots = carried
        target = jnp.where(flat_ids == expert_index, route_row, slot_count).astype(jnp.int32)
        token_at = jnp.zeros((slot_count,), jnp.int32).at[target].set(token_of_route, mode="drop")
        route_at = jnp.zeros((slot_count,), jnp.int32).at[target].set(route_index, mode="drop")
        live_slot = jnp.zeros((slot_count,), jnp.bool_).at[target].set(True, mode="drop")
        grad_rows = jnp.where(live_slot[:, None], out_grad[token_at], jnp.zeros((), jnp.bfloat16))
        prob_rows = jnp.where(live_slot, probs_half[route_at], jnp.zeros((), jnp.bfloat16)).astype(jnp.float32)
        inputs = saved_inputs[expert_index]
        gate_full = gate_weight[expert_index]
        up_full = up_weight[expert_index]
        down_full = down_weight[expert_index]
        gate_pre = jnp.dot(inputs, gate_full, preferred_element_type=jnp.float32)
        up_pre = jnp.dot(inputs, up_full, preferred_element_type=jnp.float32)
        hidden = (jax.nn.silu(gate_pre) * up_pre).astype(jnp.bfloat16)
        raw_grad = jnp.dot(grad_rows, down_full, preferred_element_type=jnp.float32)
        slot_gate = jnp.sum(raw_grad * hidden.astype(jnp.float32), axis=1).astype(jnp.bfloat16)
        scaled_grad = (prob_rows[:, None] * grad_rows.astype(jnp.float32)).astype(jnp.bfloat16)
        down_grad = jnp.dot(scaled_grad.T, hidden, preferred_element_type=jnp.float32)
        hidden_grad = prob_rows[:, None] * raw_grad
        sigmoid_gate = jax.nn.sigmoid(gate_pre)
        gate_pre_grad = (hidden_grad * up_pre * sigmoid_gate * (1.0 + gate_pre * (1.0 - sigmoid_gate))).astype(jnp.bfloat16)
        up_pre_grad = (hidden_grad * jax.nn.silu(gate_pre)).astype(jnp.bfloat16)
        slot_input = (
            jnp.dot(gate_pre_grad, gate_full.T, preferred_element_type=jnp.float32)
            + jnp.dot(up_pre_grad, up_full.T, preferred_element_type=jnp.float32)
        ).astype(jnp.bfloat16)
        gate_slots = gate_slots.at[jnp.where(live_slot, route_at, route_count).astype(jnp.int32)].set(slot_gate, mode="drop")
        input_sum = input_sum.at[jnp.where(live_slot, token_at, token_count).astype(jnp.int32)].add(slot_input.astype(jnp.float32), mode="drop")
        return (input_sum, gate_slots), down_grad

    initial = (jnp.zeros((token_count, model_width), jnp.float32), jnp.zeros((route_count,), jnp.bfloat16))
    (input_sum, gate_slots), down_grad = lax.scan(one_expert, initial, jnp.arange(expert_count, dtype=jnp.int32))
    return input_sum.astype(jnp.bfloat16), gate_slots.reshape(token_count, top_count), down_grad
```

```python
import functools

import jax
import jax.numpy as jnp
from jax import lax
from jax.experimental import pallas as pl
from jax.experimental.pallas import tpu as pltpu
from jax.sharding import PartitionSpec as P

MESH = pl.DeviceIdType.MESH
F32 = jnp.float32
BF16 = jnp.bfloat16
E = 64
PL = 16
CAP = 18
MAIN = 16
G = PL * CAP


def iota(shape, dim):
    return lax.broadcasted_iota(jnp.int32, shape, dim)


def target(me, o):
    z, y, x = me // 16, (me // 4) % 4, me % 4
    return ((z + o // 16) % 4) * 16 + ((y + (o // 4) % 4) % 4) * 4 + (x + o % 4) % 4


def kernel(
    ids_ref, prob_ref, og_ref, sin_hbm, gw_hbm, uw_hbm, dw_hbm,
    ig_ref, gg_ref, dg_hbm,
    msg, recv, xs, scr, sin, xin, wg, wu, wd, bm, cm, hid, pown, psend, precv, gpg, upg,
    msg2, rec2, wmain, wovf, gm, acc, dgv, sref, stref, ptref,
    lsem, wsem, hsem, psem, ssem, rsem, ssem2, rsem2, dsem,
):
    me = lax.axis_index("expert")
    f = lax.axis_index("fsdp")
    z = me // PL
    feat = og_ref.shape[1]
    tiles = feat // 128

    loads = [
        pltpu.make_async_copy(dw_hbm.at[0], wd, lsem.at[0]),
        pltpu.make_async_copy(sin_hbm.at[0], sin, lsem.at[1]),
        pltpu.make_async_copy(gw_hbm.at[0], wg.at[f], lsem.at[2]),
        pltpu.make_async_copy(uw_hbm.at[0], wu.at[f], lsem.at[3]),
    ]
    for c in loads[1:] + loads[:1]:
        c.start()

    barrier = pltpu.get_barrier_semaphore()

    def greet(i, carry):
        d = target(me, i)
        pl.semaphore_signal(barrier, inc=1, device_id=(d, f), device_id_type=MESH)
        pl.semaphore_signal(barrier, inc=1, device_id=(d, 1 - f), device_id_type=MESH)
        return carry

    pl.semaphore_signal(barrier, inc=1, device_id=(me, 1 - f), device_id_type=MESH)
    lax.fori_loop(1, E, greet, 0)

    lane = iota((128, 128), 1)
    row = iota((128, 128), 0)
    names = jnp.zeros((128, 128), F32)
    probs = jnp.zeros((128, 128), F32)
    for k in range(ids_ref.shape[1]):
        hit = ids_ref[:, k : k + 1] == lane
        names = names + hit.astype(F32)
        probs = probs + jnp.where(hit, prob_ref[:, k : k + 1], 0.0)
    before = (lane < row).astype(BF16)
    rank = jnp.dot(before, names.astype(BF16), preferred_element_type=F32)
    s = jnp.where(names > 0.0, rank, -1.0)
    sref[...] = s
    stref[...] = s.T
    ptref[...] = probs.astype(BF16).astype(F32).T

    st_half, pt_half = stref[...].astype(BF16), ptref[...].astype(BF16)

    def rows_of(g, carry):
        r = iota((256, 128), 0)
        spread = (r // MAIN + PL * g == iota((256, 128), 1)).astype(BF16)
        s_rep = jnp.dot(spread, st_half, preferred_element_type=F32)
        p_rep = jnp.dot(spread, pt_half, preferred_element_type=F32)
        lhs = jnp.where(s_rep == (r % MAIN).astype(F32), p_rep, 0.0).astype(BF16)
        rows = jnp.dot(lhs, og_ref[...], preferred_element_type=F32).astype(BF16)
        msg[pl.ds(PL * g, PL), :, 0:feat] = rows.reshape(PL, MAIN, feat)
        return carry

    lax.fori_loop(0, 4, rows_of, 0)
    scr[...] = jnp.zeros_like(scr)
    for c in range(CAP - MAIN):
        lhs = jnp.where(stref[0:E, :] == float(MAIN + c), ptref[0:E, :], 0.0).astype(BF16)
        rows = jnp.dot(lhs, og_ref[...], preferred_element_type=F32)
        for j in range(tiles):
            scr[pl.ds(c * tiles + j, E, stride=32), :] = rows[:, 128 * j : 128 * (j + 1)]
    packed = scr[...].reshape(E, 32, 128).astype(BF16)
    msg[:, :, feat : feat + 128] = packed[:, 0:16, :]
    msg[:, :, feat + 128 : feat + 256] = packed[:, 16:32, :]

    pl.semaphore_wait(barrier, 2 * (E - 1) + 1)

    def weight_copies():
        return [
            pltpu.make_async_remote_copy(
                src_ref=h.at[0], dst_ref=w.at[f], send_sem=wsem.at[0, i], recv_sem=wsem.at[1, i],
                device_id=(me, 1 - f), device_id_type=MESH,
            )
            for i, (h, w) in enumerate(((gw_hbm, wg), (uw_hbm, wu)))
        ]

    for c in weight_copies():
        c.start()

    def dispatch(i, carry):
        d = target(me, (i * 23) % E)
        pltpu.make_async_remote_copy(
            src_ref=msg.at[d], dst_ref=recv.at[me], send_sem=ssem.at[0], recv_sem=rsem.at[z],
            device_id=(d, f), device_id_type=MESH,
        ).start()
        return carry

    lax.fori_loop(1, E, dispatch, 0)
    pltpu.make_async_copy(msg.at[me], recv.at[me], rsem.at[z]).start()

    s_half = sref[...].astype(BF16)
    for g in range(4):
        r = iota((128, 256), 1)
        spread = (r // MAIN + PL * g == iota((128, 256), 0)).astype(BF16)
        s_rep = jnp.dot(s_half, spread, preferred_element_type=F32)
        wmain[g] = (s_rep == (r % MAIN).astype(F32)).astype(BF16)
        r = iota((128, 32), 1)
        spread = (r % PL + PL * g == iota((128, 32), 0)).astype(BF16)
        s_rep = jnp.dot(s_half, spread, preferred_element_type=F32)
        wovf[g] = (s_rep == (MAIN + r // PL).astype(F32)).astype(BF16)

    loads[1].wait()
    r = iota((G, G), 0)
    origin = jnp.where(
        r < PL * MAIN, CAP * (r // MAIN) + r % MAIN,
        CAP * ((r - PL * MAIN) % PL) + MAIN + (r - PL * MAIN) // PL,
    )
    perm = (origin == iota((G, G), 1)).astype(BF16)
    for q in range(2):
        for n in range(0, 2 * feat, 512):
            xin[q, :, n : n + 512] = jnp.dot(
                perm, sin[G * q : G * (q + 1), n : n + 512], preferred_element_type=F32
            ).astype(BF16)

    loads[2].wait()
    loads[3].wait()
    for c in weight_copies():
        c.wait()
    for n in range(0, wd.shape[1], 256):
        cols = slice(n, n + 256)

        def gated(q, carry):
            a, b = xin[q, :, 0:feat], xin[q, :, feat : 2 * feat]
            gate = jnp.dot(a, wg[0, :, cols], preferred_element_type=F32) + jnp.dot(
                b, wg[1, :, cols], preferred_element_type=F32
            )
            up = jnp.dot(a, wu[0, :, cols], preferred_element_type=F32) + jnp.dot(
                b, wu[1, :, cols], preferred_element_type=F32
            )
            sg = jax.nn.sigmoid(gate)
            silu = gate * sg
            cm[q, :, cols] = silu
            bm[q, :, cols] = up * sg * (1.0 + gate * (1.0 - sg))
            hid[f, q, :, cols] = (silu * up).astype(BF16)
            return carry

        lax.fori_loop(0, 2, gated, 0)

    hid_copy = pltpu.make_async_remote_copy(
        src_ref=hid.at[f], dst_ref=hid.at[f], send_sem=hsem.at[0], recv_sem=hsem.at[1],
        device_id=(me, 1 - f), device_id_type=MESH,
    )
    hid_copy.start()

    def overflow_rows(ref, g):
        tail = ref[pl.ds(PL * g, PL), :, feat : feat + 256].astype(F32)
        for h in range(2):
            scr[pl.ds(PL * MAIN * h, PL * MAIN), :] = tail[:, :, 128 * h : 128 * (h + 1)].reshape(
                PL * MAIN, 128
            )

        def piece(i):
            return scr[pl.ds(PL * MAIN * (i // MAIN) + i % MAIN, PL, stride=MAIN), :]

        return [
            jnp.concatenate([piece(c * tiles + j) for j in range(tiles)], axis=1) for c in range(CAP - MAIN)
        ], piece

    def unpack(i, carry):
        g = (z + i) % 4
        slab = recv.at[pl.ds(PL * g, PL)]
        pltpu.make_async_copy(slab, slab, rsem.at[g]).wait()
        xs[g, 0 : PL * MAIN, :] = recv[pl.ds(PL * g, PL), :, 0:feat].reshape(PL * MAIN, feat)
        ovf, _ = overflow_rows(recv, g)
        xs[g, PL * MAIN : G, :] = jnp.concatenate(ovf, axis=0).astype(BF16)
        return carry

    lax.fori_loop(0, 4, unpack, 0)
    loads[0].wait()

    def partial_copy(q):
        return pltpu.make_async_remote_copy(
            src_ref=psend.at[q], dst_ref=precv.at[q], send_sem=psem.at[0, q], recv_sem=psem.at[1, q],
            device_id=(me, 1 - f), device_id_type=MESH,
        )

    def other(q, carry):
        psend[q] = jnp.dot(xs[2 * (1 - f) + q], wd[...], preferred_element_type=F32)
        partial_copy(q).start()
        return carry

    lax.fori_loop(0, 2, other, 0)

    def own(q, carry):
        pown[q] = jnp.dot(xs[2 * f + q], wd[...], preferred_element_type=F32)
        return carry

    lax.fori_loop(0, 2, own, 0)

    def back(i, carry):
        q = (i + z) % 2
        partial_copy(q).wait_recv()
        raw = pown[q] + precv[q]
        gpg[...] = (raw * bm[q]).astype(BF16)
        upg[...] = (raw * cm[q]).astype(BF16)
        gates = jnp.sum(raw * hid[f, q].astype(F32), axis=1, keepdims=True)
        r, ln = iota((PL * MAIN, 128), 0), iota((PL * MAIN, 128), 1)
        table = jnp.where(ln == r % MAIN, gates[0 : PL * MAIN], 0.0).reshape(PL, MAIN, 128).sum(axis=1)
        r, ln = iota((G - PL * MAIN, 128), 0), iota((G - PL * MAIN, 128), 1)
        table = table + jnp.where(ln == MAIN + r // PL, gates[PL * MAIN : G], 0.0).reshape(
            CAP - MAIN, PL, 128
        ).sum(axis=0)
        for h in range(2):
            out = msg2.at[q, h]
            for n in range(0, feat, 256):
                rows = lax.dot_general(
                    gpg[...], wg[h, n : n + 256, :], (((1,), (1,)), ((), ())), preferred_element_type=F32
                ) + lax.dot_general(
                    upg[...], wu[h, n : n + 256, :], (((1,), (1,)), ((), ())), preferred_element_type=F32
                )
                out[:, :, n : n + 256] = rows[0 : PL * MAIN].astype(BF16).reshape(PL, MAIN, 256)
                for c in range(CAP - MAIN):
                    for jj in range(2):
                        scr[pl.ds(c * tiles + n // 128 + jj, PL, stride=32), :] = rows[
                            PL * (MAIN + c) : PL * (MAIN + c + 1), 128 * jj : 128 * (jj + 1)
                        ]
            scr[pl.ds(2 * tiles, PL, stride=32), :] = table
            packed = scr[0 : PL * 32, :].reshape(PL, 32, 128).astype(BF16)
            out[:, :, feat : feat + 128] = packed[:, 0:16, :]
            out[:, :, feat + 128 : feat + 256] = packed[:, 16:32, :]

            def send(j, carry):
                blk = PL * (2 * f + q) + (me % PL + 7 * j) % PL
                here = jnp.logical_and(blk == me, h == f)

                @pl.when(here)
                def _():
                    pltpu.make_async_copy(out.at[blk % PL], rec2.at[me], rsem2.at[z]).start()

                @pl.when(jnp.logical_not(here))
                def _():
                    pltpu.make_async_remote_copy(
                        src_ref=out.at[blk % PL], dst_ref=rec2.at[me], send_sem=ssem2.at[q, h],
                        recv_sem=rsem2.at[z], device_id=(blk, h), device_id_type=MESH,
                    ).start()

                return carry

            lax.fori_loop(0, PL, send, 0)
        return carry

    lax.fori_loop(0, 2, back, 0)

    hid_copy.wait()
    inner = hid.shape[3]

    def down(m, carry):
        at = pl.multiple_of(m * 256, 256)
        lhs = xs[:, :, pl.ds(at, 256)].reshape(4 * G, 256)
        dgv[m] = lax.dot_general(
            lhs, hid[...].reshape(4 * G, inner), (((0,), (0,)), ((), ())), preferred_element_type=F32
        )
        pltpu.make_async_copy(dgv.at[m], dg_hbm.at[0, pl.ds(at, 256), :], dsem.at[m]).start()
        return carry

    lax.fori_loop(0, feat // 256, down, 0)

    acc[...] = jnp.zeros_like(acc)

    def home(i, carry):
        g = (z + i) % 4
        slab = rec2.at[pl.ds(PL * g, PL)]
        pltpu.make_async_copy(slab, slab, rsem2.at[g]).wait()
        ovf, piece = overflow_rows(rec2, g)
        gm[pl.ds(PL * g, PL), :] = piece(2 * tiles)
        acc[...] += jnp.dot(
            wmain[g], rec2[pl.ds(PL * g, PL), :, 0:feat].reshape(PL * MAIN, feat), preferred_element_type=F32
        ) + jnp.dot(wovf[g], jnp.concatenate(ovf, axis=0).astype(BF16), preferred_element_type=F32)
        return carry

    lax.fori_loop(0, 4, home, 0)
    ig_ref[...] = acc[...].astype(BF16)

    gates = jnp.zeros((128, 128), F32)
    table = gm[...].astype(BF16)
    for k in range(ids_ref.shape[1]):
        hit = ids_ref[:, k : k + 1] == lane
        slot = jnp.sum(jnp.where(hit, sref[...], 0.0), axis=1, keepdims=True)
        line = jnp.dot(hit.astype(BF16)[:, 0:E], table, preferred_element_type=F32)
        value = jnp.sum(jnp.where(lane.astype(F32) == slot, line, 0.0), axis=1, keepdims=True)
        value = value / prob_ref[:, k : k + 1].astype(BF16).astype(F32)
        gates = jnp.where(lane == k, value, gates)
    gg_ref[...] = gates[:, 0 : ids_ref.shape[1]].astype(BF16)

    most = msg.at[pl.ds(0, E - 1)]
    pltpu.make_async_copy(most, most, ssem.at[0]).wait()
    for q in range(2):
        partial_copy(q).wait_send()
        for h in range(2):
            local = jnp.logical_and(z == 2 * f + q, f == h)

            @pl.when(local)
            def _():
                part = msg2.at[q, h, pl.ds(0, PL - 1)]
                pltpu.make_async_copy(part, part, ssem2.at[q, h]).wait()

            @pl.when(jnp.logical_not(local))
            def _():
                pltpu.make_async_copy(msg2.at[q, h], msg2.at[q, h], ssem2.at[q, h]).wait()

    def flush(m, carry):
        at = pl.multiple_of(m * 256, 256)
        pltpu.make_async_copy(dgv.at[m], dg_hbm.at[0, pl.ds(at, 256), :], dsem.at[m]).wait()
        return carry

    lax.fori_loop(0, feat // 256, flush, 0)


def body(out_grad, expert_ids, gate_probs, saved_inputs, gate_weight, up_weight, down_weight):
    tokens, feat = out_grad.shape
    top = expert_ids.shape[1]
    hidden = down_weight.shape[2]
    wide = feat + 256
    dma = pltpu.SemaphoreType.DMA
    vmem = pl.BlockSpec(memory_space=pltpu.VMEM)
    hbm = pl.BlockSpec(memory_space=pl.ANY)
    return pl.pallas_call(
        kernel,
        out_shape=(
            jax.ShapeDtypeStruct((tokens, feat), BF16),
            jax.ShapeDtypeStruct((tokens, top), BF16),
            jax.ShapeDtypeStruct((1, feat, hidden), F32),
        ),
        in_specs=[vmem, vmem, vmem, hbm, hbm, hbm, hbm],
        out_specs=(vmem, vmem, hbm),
        scratch_shapes=[
            pltpu.VMEM((E, MAIN, wide), BF16),
            pltpu.VMEM((E, MAIN, wide), BF16),
            pltpu.VMEM((4, G, feat), BF16),
            pltpu.VMEM((E * 32, 128), F32),
            pltpu.VMEM((2 * G, 2 * feat), BF16),
            pltpu.VMEM((2, G, 2 * feat), BF16),
            pltpu.VMEM((2, feat, hidden), BF16),
            pltpu.VMEM((2, feat, hidden), BF16),
            pltpu.VMEM((feat, hidden), BF16),
            pltpu.VMEM((2, G, hidden), F32),
            pltpu.VMEM((2, G, hidden), F32),
            pltpu.VMEM((2, 2, G, hidden), BF16),
            pltpu.VMEM((2, G, hidden), F32),
            pltpu.VMEM((2, G, hidden), F32),
            pltpu.VMEM((2, G, hidden), F32),
            pltpu.VMEM((G, hidden), BF16),
            pltpu.VMEM((G, hidden), BF16),
            pltpu.VMEM((2, 2, PL, MAIN, wide), BF16),
            pltpu.VMEM((E, MAIN, wide), BF16),
            pltpu.VMEM((4, tokens, PL * MAIN), BF16),
            pltpu.VMEM((4, tokens, G - PL * MAIN), BF16),
            pltpu.VMEM((E, 128), F32),
            pltpu.VMEM((tokens, feat), F32),
            pltpu.VMEM((feat // 256, 256, hidden), F32),
            pltpu.VMEM((tokens, 128), F32),
            pltpu.VMEM((128, tokens), F32),
            pltpu.VMEM((128, tokens), F32),
            dma((4,)),
            dma((2, 2)),
            dma((2,)),
            dma((2, 2)),
            dma((1,)),
            dma((4,)),
            dma((2, 2)),
            dma((4,)),
            dma((feat // 256,)),
        ],
        compiler_params=pltpu.CompilerParams(
            collective_id=0, has_side_effects=True, vmem_limit_bytes=62 << 20
        ),
    )(expert_ids, gate_probs, out_grad, saved_inputs, gate_weight, up_weight, down_weight)


def solution(mesh):
    placed = (
        P("expert", "fsdp"),
        P("expert", None),
        P("expert", None),
        P("expert", "fsdp", None),
        P("expert", "fsdp", None),
        P("expert", "fsdp", None),
        P("expert", "fsdp", None),
    )
    return jax.shard_map(
        body,
        mesh=mesh,
        in_specs=placed,
        out_specs=(P("expert", "fsdp"), P("expert", None), P("expert", "fsdp", None)),
        check_vma=False,
    )
```

```python
import functools

import jax
import jax.numpy as jnp
from jax import lax
from jax.experimental import pallas as pl
from jax.experimental.pallas import tpu as pltpu
from jax.sharding import PartitionSpec as P

MESH = pl.DeviceIdType.MESH
F32 = jnp.float32
BF16 = jnp.bfloat16
E = 64
PL = 16
CAP = 18
MAIN = 16
G = PL * CAP


def iota(shape, dim):
    return lax.broadcasted_iota(jnp.int32, shape, dim)


def target(me, o):
    z, y, x = me // 16, (me // 4) % 4, me % 4
    return ((z + o // 16) % 4) * 16 + ((y + (o // 4) % 4) % 4) * 4 + (x + o % 4) % 4


def near(me, f, dz, yx):
    sign = 1 - 2 * f
    z = (me // 16 + 4 + sign * dz) % 4
    y = ((me // 4) % 4 + 4 + sign * (yx // 4)) % 4
    x = (me % 4 + 4 + sign * (yx % 4)) % 4
    return z * 16 + y * 4 + x


def kernel(
    ids_ref, prob_ref, og_ref, sin_hbm, gw_hbm, uw_hbm, dw_hbm,
    ig_ref, gg_ref, dgv,
    msg, recv, xs, scr, sin, xin, wg, wu, wd, bm, cm, hid, pown, psend, precv, gpg, upg,
    msg2, rec2, wmain, wovf, gm, acc, sref, stref, ptref,
    lsem, wsem, hsem, psem, ssem, rsem, ssem2, rsem2,
):
    me = lax.axis_index("expert")
    f = lax.axis_index("fsdp")
    z = me // PL
    feat = og_ref.shape[1]
    tiles = feat // 128
    top = ids_ref.shape[0]

    loads = [
        pltpu.make_async_copy(sin_hbm.at[0], sin, lsem.at[0]),
        pltpu.make_async_copy(gw_hbm.at[0], wg.at[f], lsem.at[1]),
        pltpu.make_async_copy(uw_hbm.at[0], wu.at[f], lsem.at[2]),
        pltpu.make_async_copy(dw_hbm.at[0], wd, lsem.at[3]),
    ]
    for c in loads:
        c.start()

    barrier = pltpu.get_barrier_semaphore()

    def greet(i, carry):
        d = target(me, i)
        pl.semaphore_signal(barrier, inc=1, device_id=(d, f), device_id_type=MESH)
        pl.semaphore_signal(barrier, inc=1, device_id=(d, 1 - f), device_id_type=MESH)
        return carry

    lax.fori_loop(1, E, greet, 0)
    pl.semaphore_signal(barrier, inc=1, device_id=(me, 1 - f), device_id_type=MESH)

    lane = iota((128, 128), 1)
    row = iota((128, 128), 0)
    names = jnp.zeros((128, 128), F32)
    probs = jnp.zeros((128, 128), F32)
    for k in range(top):
        hit = ids_ref[k : k + 1, :] == row
        names = names + hit.astype(F32)
        probs = probs + jnp.where(hit, prob_ref[k : k + 1, :], 0.0)
    before = (row < lane).astype(BF16)
    rank = jnp.dot(names.astype(BF16), before, preferred_element_type=F32)
    stref[...] = jnp.where(names > 0.0, rank, -1.0)
    ptref[...] = probs

    def place(r):
        main = r < PL * MAIN
        over = r - PL * MAIN
        return jnp.where(main, r // MAIN, over % PL), jnp.where(main, r % MAIN, MAIN + over // PL)

    def pack(ref):
        packed = scr[0 : PL * 32, :].reshape(PL, 32, 128).astype(BF16)
        ref[:, :, feat : feat + 128] = packed[:, 0:16, :]
        ref[:, :, feat + 128 : feat + 256] = packed[:, 16:32, :]

    def build(g):
        who, slot = place(iota((G, 128), 0))
        spread = (who + PL * g == iota((G, 128), 1)).astype(BF16)
        s_rep = jnp.dot(spread, stref[...].astype(BF16), preferred_element_type=F32)
        p_rep = jnp.dot(spread, ptref[...].astype(BF16), preferred_element_type=F32)
        lhs = jnp.where(s_rep == slot.astype(F32), p_rep, 0.0).astype(BF16)
        out = msg.at[pl.ds(PL * g, PL)]
        for n in range(0, feat, 256):
            rows = jnp.dot(lhs, og_ref[:, n : n + 256], preferred_element_type=F32)
            out[:, :, n : n + 256] = rows[0 : PL * MAIN].astype(BF16).reshape(PL, MAIN, 256)
            for c in range(CAP - MAIN):
                for j in range(2):
                    scr[pl.ds(c * tiles + n // 128 + j, PL, stride=32), :] = rows[
                        PL * (MAIN + c) : PL * (MAIN + c + 1), 128 * j : 128 * (j + 1)
                    ]
        pack(out)

    def dispatch(phase):
        def step(i, carry):
            d = near(me, f, 1 - phase + 2 * (i % 2), ((i // 2) * 7) % PL)
            pltpu.make_async_remote_copy(
                src_ref=msg.at[d], dst_ref=recv.at[me], send_sem=ssem.at[0], recv_sem=rsem.at[z],
                device_id=(d, f), device_id_type=MESH,
            ).start()
            return carry

        lax.fori_loop(phase, 32, step, 0)

    def weight_copies():
        return [
            pltpu.make_async_remote_copy(
                src_ref=h.at[0], dst_ref=w.at[f], send_sem=wsem.at[0, i], recv_sem=wsem.at[1, i],
                device_id=(me, 1 - f), device_id_type=MESH,
            )
            for i, (h, w) in enumerate(((gw_hbm, wg), (uw_hbm, wu)))
        ]

    scr[...] = jnp.zeros_like(scr)

    def build_odd(i, carry):
        build((z + 1 + 2 * i) % 4)
        return carry

    lax.fori_loop(0, 2, build_odd, 0)
    pl.semaphore_wait(barrier, 2 * (E - 1) + 1)
    dispatch(0)
    for c in weight_copies():
        c.start()

    def build_even(i, carry):
        build((z + 2 * i) % 4)
        return carry

    lax.fori_loop(0, 2, build_even, 0)
    dispatch(1)
    pltpu.make_async_copy(msg.at[me], recv.at[me], rsem.at[z]).start()

    sref[...] = stref[...].T
    s_half = sref[...].astype(BF16)
    for g in range(4):
        who, slot = place(iota((128, G), 1))
        spread = (who + PL * g == iota((128, G), 0)).astype(BF16)
        s_rep = jnp.dot(s_half, spread, preferred_element_type=F32)
        hot = (s_rep == slot.astype(F32)).astype(BF16)
        wmain[g] = hot[:, 0 : PL * MAIN]
        wovf[g] = hot[:, PL * MAIN : G]

    loads[0].wait()
    who, slot = place(iota((G, G), 0))
    perm = (CAP * who + slot == iota((G, G), 1)).astype(BF16)
    for q in range(2):
        for n in range(0, 2 * feat, 512):
            xin[q, :, n : n + 512] = jnp.dot(
                perm, sin[G * q : G * (q + 1), n : n + 512], preferred_element_type=F32
            ).astype(BF16)

    loads[1].wait()
    loads[2].wait()
    for c in weight_copies():
        c.wait()
    for n in range(0, wd.shape[1], 256):
        cols = slice(n, n + 256)

        def gated(q, carry):
            a, b = xin[q, :, 0:feat], xin[q, :, feat : 2 * feat]
            gate = jnp.dot(a, wg[0, :, cols], preferred_element_type=F32) + jnp.dot(
                b, wg[1, :, cols], preferred_element_type=F32
            )
            up = jnp.dot(a, wu[0, :, cols], preferred_element_type=F32) + jnp.dot(
                b, wu[1, :, cols], preferred_element_type=F32
            )
            sg = jax.nn.sigmoid(gate)
            silu = gate * sg
            cm[q, :, cols] = silu
            bm[q, :, cols] = up * sg * (1.0 + gate * (1.0 - sg))
            hid[f, q, :, cols] = (silu * up).astype(BF16)
            return carry

        lax.fori_loop(0, 2, gated, 0)

    hid_copy = pltpu.make_async_remote_copy(
        src_ref=hid.at[f], dst_ref=hid.at[f], send_sem=hsem.at[0], recv_sem=hsem.at[1],
        device_id=(me, 1 - f), device_id_type=MESH,
    )
    hid_copy.start()
    loads[3].wait()

    def overflow_rows(ref, g):
        tail = ref[pl.ds(PL * g, PL), :, feat : feat + 256].astype(F32)
        for h in range(2):
            scr[pl.ds(PL * MAIN * h, PL * MAIN), :] = tail[:, :, 128 * h : 128 * (h + 1)].reshape(
                PL * MAIN, 128
            )

        def piece(i):
            return scr[pl.ds(PL * MAIN * (i // MAIN) + i % MAIN, PL, stride=MAIN), :]

        return [
            jnp.concatenate([piece(c * tiles + j) for j in range(tiles)], axis=1) for c in range(CAP - MAIN)
        ], piece

    def unpack(g):
        slab = recv.at[pl.ds(PL * g, PL)]
        pltpu.make_async_copy(slab, slab, rsem.at[g]).wait()
        xs[g, 0 : PL * MAIN, :] = recv[pl.ds(PL * g, PL), :, 0:feat].reshape(PL * MAIN, feat)
        ovf, _ = overflow_rows(recv, g)
        xs[g, PL * MAIN : G, :] = jnp.concatenate(ovf, axis=0).astype(BF16)

    def partial_copy(q):
        return pltpu.make_async_remote_copy(
            src_ref=psend.at[q], dst_ref=precv.at[q], send_sem=psem.at[0, q], recv_sem=psem.at[1, q],
            device_id=(me, 1 - f), device_id_type=MESH,
        )

    def back(i, carry):
        q = (z + 1 + i) % 2
        unpack(2 * (1 - f) + q)
        psend[q] = jnp.dot(xs[2 * (1 - f) + q], wd[...], preferred_element_type=F32)
        partial_copy(q).start()
        unpack(2 * f + q)
        pown[...] = jnp.dot(xs[2 * f + q], wd[...], preferred_element_type=F32)
        partial_copy(q).wait_recv()
        raw = pown[...] + precv[q]
        gpg[...] = (raw * bm[q]).astype(BF16)
        upg[...] = (raw * cm[q]).astype(BF16)
        gates = jnp.sum(raw * hid[f, q].astype(F32), axis=1, keepdims=True)
        r, ln = iota((PL * MAIN, 128), 0), iota((PL * MAIN, 128), 1)
        table = jnp.where(ln == r % MAIN, gates[0 : PL * MAIN], 0.0).reshape(PL, MAIN, 128).sum(axis=1)
        r, ln = iota((G - PL * MAIN, 128), 0), iota((G - PL * MAIN, 128), 1)
        table = table + jnp.where(ln == MAIN + r // PL, gates[PL * MAIN : G], 0.0).reshape(
            CAP - MAIN, PL, 128
        ).sum(axis=0)
        for h in range(2):
            out = msg2.at[q, h]
            for n in range(0, feat, 256):
                rows = lax.dot_general(
                    gpg[...], wg[h, n : n + 256, :], (((1,), (1,)), ((), ())), preferred_element_type=F32
                ) + lax.dot_general(
                    upg[...], wu[h, n : n + 256, :], (((1,), (1,)), ((), ())), preferred_element_type=F32
                )
                out[:, :, n : n + 256] = rows[0 : PL * MAIN].astype(BF16).reshape(PL, MAIN, 256)
                for c in range(CAP - MAIN):
                    for jj in range(2):
                        scr[pl.ds(c * tiles + n // 128 + jj, PL, stride=32), :] = rows[
                            PL * (MAIN + c) : PL * (MAIN + c + 1), 128 * jj : 128 * (jj + 1)
                        ]
            scr[pl.ds(2 * tiles, PL, stride=32), :] = table
            pack(out)

            def send(j, carry):
                blk = near((2 * f + q) * PL + me % PL, f, 0, (j * 7) % PL)
                here = jnp.logical_and(blk == me, h == f)

                @pl.when(here)
                def _():
                    pltpu.make_async_copy(out.at[blk % PL], rec2.at[me], rsem2.at[z]).start()

                @pl.when(jnp.logical_not(here))
                def _():
                    pltpu.make_async_remote_copy(
                        src_ref=out.at[blk % PL], dst_ref=rec2.at[me], send_sem=ssem2.at[q, h],
                        recv_sem=rsem2.at[z], device_id=(blk, h), device_id_type=MESH,
                    ).start()

                return carry

            lax.fori_loop(0, PL, send, 0)
        return carry

    lax.fori_loop(0, 2, back, 0)

    hid_copy.wait()
    inner = hid.shape[3]

    def down(m, carry):
        at = pl.multiple_of(m * 256, 256)
        lhs = xs[:, :, pl.ds(at, 256)].reshape(4 * G, 256)
        dgv[0, pl.ds(at, 256), :] = lax.dot_general(
            lhs, hid[...].reshape(4 * G, inner), (((0,), (0,)), ((), ())), preferred_element_type=F32
        )
        return carry

    lax.fori_loop(0, feat // 256, down, 0)

    acc[...] = jnp.zeros_like(acc)

    def home(i, carry):
        g = (z + 1 + 2 * i - 3 * (i // 2)) % 4
        slab = rec2.at[pl.ds(PL * g, PL)]
        pltpu.make_async_copy(slab, slab, rsem2.at[g]).wait()
        ovf, piece = overflow_rows(rec2, g)
        gm[pl.ds(PL * g, PL), :] = piece(2 * tiles)
        acc[...] += jnp.dot(
            wmain[g], rec2[pl.ds(PL * g, PL), :, 0:feat].reshape(PL * MAIN, feat), preferred_element_type=F32
        ) + jnp.dot(wovf[g], jnp.concatenate(ovf, axis=0).astype(BF16), preferred_element_type=F32)
        return carry

    lax.fori_loop(0, 4, home, 0)
    ig_ref[...] = acc[...].astype(BF16)

    table = gm[...].astype(BF16)
    values = jnp.zeros((8, 128), F32)
    for k in range(top):
        hit = ids_ref[k : k + 1, :] == row
        slot = jnp.sum(jnp.where(hit, stref[...], 0.0), axis=0, keepdims=True)
        line = lax.dot_general(
            table, hit.astype(BF16)[0:E, :], (((0,), (0,)), ((), ())), preferred_element_type=F32
        )
        value = jnp.sum(jnp.where(row.astype(F32) == slot, line, 0.0), axis=0, keepdims=True)
        value = value / prob_ref[k : k + 1, :].astype(BF16).astype(F32)
        values = jnp.where(row[0:8] == k, value, values)
    gg_ref[...] = values[0:top].astype(BF16)

    most = msg.at[pl.ds(0, E - 1)]
    pltpu.make_async_copy(most, most, ssem.at[0]).wait()
    for q in range(2):
        partial_copy(q).wait_send()
        for h in range(2):
            local = jnp.logical_and(z == 2 * f + q, f == h)

            @pl.when(local)
            def _():
                part = msg2.at[q, h, pl.ds(0, PL - 1)]
                pltpu.make_async_copy(part, part, ssem2.at[q, h]).wait()

            @pl.when(jnp.logical_not(local))
            def _():
                pltpu.make_async_copy(msg2.at[q, h], msg2.at[q, h], ssem2.at[q, h]).wait()


def body(out_grad, expert_ids, gate_probs, saved_inputs, gate_weight, up_weight, down_weight):
    tokens, feat = out_grad.shape
    top = expert_ids.shape[1]
    hidden = down_weight.shape[2]
    wide = feat + 256
    dma = pltpu.SemaphoreType.DMA
    vmem = pl.BlockSpec(memory_space=pltpu.VMEM)
    hbm = pl.BlockSpec(memory_space=pl.ANY)
    input_grad, gate_grad, down_grad = pl.pallas_call(
        kernel,
        out_shape=(
            pltpu.VMEM((tokens, feat), BF16),
            pltpu.VMEM((top, tokens), BF16),
            pltpu.VMEM((1, feat, hidden), F32),
        ),
        in_specs=[vmem, vmem, vmem, hbm, hbm, hbm, hbm],
        out_specs=(vmem, vmem, vmem),
        scratch_shapes=[
            pltpu.VMEM((E, MAIN, wide), BF16),
            pltpu.VMEM((E, MAIN, wide), BF16),
            pltpu.VMEM((4, G, feat), BF16),
            pltpu.VMEM((E * 32, 128), F32),
            pltpu.VMEM((2 * G, 2 * feat), BF16),
            pltpu.VMEM((2, G, 2 * feat), BF16),
            pltpu.VMEM((2, feat, hidden), BF16),
            pltpu.VMEM((2, feat, hidden), BF16),
            pltpu.VMEM((feat, hidden), BF16),
            pltpu.VMEM((2, G, hidden), F32),
            pltpu.VMEM((2, G, hidden), F32),
            pltpu.VMEM((2, 2, G, hidden), BF16),
            pltpu.VMEM((G, hidden), F32),
            pltpu.VMEM((2, G, hidden), F32),
            pltpu.VMEM((2, G, hidden), F32),
            pltpu.VMEM((G, hidden), BF16),
            pltpu.VMEM((G, hidden), BF16),
            pltpu.VMEM((2, 2, PL, MAIN, wide), BF16),
            pltpu.VMEM((E, MAIN, wide), BF16),
            pltpu.VMEM((4, tokens, PL * MAIN), BF16),
            pltpu.VMEM((4, tokens, G - PL * MAIN), BF16),
            pltpu.VMEM((E, 128), F32),
            pltpu.VMEM((tokens, feat), F32),
            pltpu.VMEM((tokens, 128), F32),
            pltpu.VMEM((128, tokens), F32),
            pltpu.VMEM((128, tokens), F32),
            dma((4,)),
            dma((2, 2)),
            dma((2,)),
            dma((2, 2)),
            dma((1,)),
            dma((4,)),
            dma((2, 2)),
            dma((4,)),
        ],
        compiler_params=pltpu.CompilerParams(
            collective_id=0, has_side_effects=True, vmem_limit_bytes=50 << 20
        ),
    )(expert_ids.T, gate_probs.T, out_grad, saved_inputs, gate_weight, up_weight, down_weight)
    return input_grad, gate_grad.T, down_grad


def solution(mesh):
    placed = (
        P("expert", "fsdp"),
        P("expert", None),
        P("expert", None),
        P("expert", "fsdp", None),
        P("expert", "fsdp", None),
        P("expert", "fsdp", None),
        P("expert", "fsdp", None),
    )
    return jax.shard_map(
        body,
        mesh=mesh,
        in_specs=placed,
        out_specs=(P("expert", "fsdp"), P("expert", None), P("expert", "fsdp", None)),
        check_vma=False,
    )
```

```python
import functools

import jax
import jax.numpy as jnp
from jax import lax
from jax.experimental import pallas as pl
from jax.experimental.pallas import tpu as pltpu
from jax.sharding import PartitionSpec as P

MESH = pl.DeviceIdType.MESH
F32 = jnp.float32
BF16 = jnp.bfloat16
E = 64
PL = 16
CAP = 18
MAIN = 16
REST = CAP - MAIN
G = PL * CAP


def iota(shape, dim):
    return lax.broadcasted_iota(jnp.int32, shape, dim)


def near(me, f, dz, yx):
    sign = 1 - 2 * f
    z = (me // 16 + 4 + sign * dz) % 4
    y = ((me // 4) % 4 + 4 + sign * (yx // 4)) % 4
    x = (me % 4 + 4 + sign * (yx % 4)) % 4
    return z * 16 + y * 4 + x


def kernel(
    ids_ref, prob_ref, og_ref, sin_hbm, gw_hbm, uw_hbm, dw_hbm,
    ig_ref, gg_ref, dgv,
    msg, over, recv, recvo, xs, sin, xin, wg, wu, wd, bm, cm, hid, pown, psend, precv, gpg, upg,
    msg2, over2, rec2, rec2o, wmain, wovf, gm, acc, sref, stref, ptref,
    lsem, wsem, hsem, psem, ssem, rsem, ssem2, rsem2, met,
):
    me = lax.axis_index("expert")
    f = lax.axis_index("fsdp")
    z = me // PL
    feat = og_ref.shape[1]
    top = ids_ref.shape[0]

    loads = [
        pltpu.make_async_copy(sin_hbm.at[0], sin, lsem.at[0]),
        pltpu.make_async_copy(gw_hbm.at[0], wg.at[f], lsem.at[1]),
        pltpu.make_async_copy(uw_hbm.at[0], wu.at[f], lsem.at[2]),
        pltpu.make_async_copy(dw_hbm.at[0], wd, lsem.at[3]),
    ]
    for c in loads:
        c.start()

    barrier = pltpu.get_barrier_semaphore()

    def greet(i, carry):
        d = near(me, f, 1 + 2 * (i % 2), i // 2)
        pl.semaphore_signal(barrier, inc=1, device_id=(d, f), device_id_type=MESH)
        return carry

    lax.fori_loop(0, 32, greet, 0)
    pl.semaphore_signal(barrier, inc=1, device_id=(me, 1 - f), device_id_type=MESH)

    lane = iota((128, 128), 1)
    row = iota((128, 128), 0)
    names = jnp.zeros((128, 128), F32)
    probs = jnp.zeros((128, 128), F32)
    for k in range(top):
        hit = ids_ref[k : k + 1, :] == row
        names = names + hit.astype(F32)
        probs = probs + jnp.where(hit, prob_ref[k : k + 1, :], 0.0)
    before = (row < lane).astype(BF16)
    rank = jnp.dot(names.astype(BF16), before, preferred_element_type=F32)
    stref[...] = jnp.where(names > 0.0, rank, -1.0)
    ptref[...] = probs

    def place(r):
        main = r < PL * MAIN
        rest = r - PL * MAIN
        return jnp.where(main, r // MAIN, rest // REST), jnp.where(main, r % MAIN, MAIN + rest % REST)

    def build(g):
        who, slot = place(iota((G, 128), 0))
        spread = (who + PL * g == iota((G, 128), 1)).astype(BF16)
        s_rep = jnp.dot(spread, stref[...].astype(BF16), preferred_element_type=F32)
        p_rep = jnp.dot(spread, ptref[...].astype(BF16), preferred_element_type=F32)
        lhs = jnp.where(s_rep == slot.astype(F32), p_rep, 0.0).astype(BF16)
        for n in range(0, feat, 256):
            rows = jnp.dot(lhs, og_ref[:, n : n + 256], preferred_element_type=F32).astype(BF16)
            msg[pl.ds(PL * g, PL), :, n : n + 256] = rows[0 : PL * MAIN].reshape(PL, MAIN, 256)
            over[pl.ds(PL * g, PL), :, n : n + 256] = rows[PL * MAIN : G].reshape(PL, REST, 256)

    def dispatch(phase):
        def step(i, carry):
            j = (i * 5) % 32
            d = near(me, f, 1 - phase + 2 * (j // PL), j % PL)
            for b, (src, dst) in enumerate(((msg, recv), (over, recvo))):
                pltpu.make_async_remote_copy(
                    src_ref=src.at[d], dst_ref=dst.at[me], send_sem=ssem.at[b], recv_sem=rsem.at[b, z],
                    device_id=(d, f), device_id_type=MESH,
                ).start()
            return carry

        lax.fori_loop(phase, 32, step, 0)

    def weight_copies():
        return [
            pltpu.make_async_remote_copy(
                src_ref=h.at[0], dst_ref=w.at[f], send_sem=wsem.at[0, i], recv_sem=wsem.at[1, i],
                device_id=(me, 1 - f), device_id_type=MESH,
            )
            for i, (h, w) in enumerate(((gw_hbm, wg), (uw_hbm, wu)))
        ]

    def build_odd(i, carry):
        build((z + 1 + 2 * i) % 4)
        return carry

    lax.fori_loop(0, 2, build_odd, 0)
    pl.semaphore_wait(barrier, 33)
    pl.semaphore_signal(met.at[0], inc=1, device_id=((me + PL) % E, f), device_id_type=MESH)
    dispatch(0)
    for c in weight_copies():
        c.start()

    def build_even(i, carry):
        build((z + 2 * i) % 4)
        return carry

    lax.fori_loop(0, 2, build_even, 0)
    pl.semaphore_wait(met.at[0], 1)
    pl.semaphore_signal(met.at[1], inc=1, device_id=(me, 1 - f), device_id_type=MESH)
    dispatch(1)
    pltpu.make_async_copy(msg.at[me], recv.at[me], rsem.at[0, z]).start()
    pltpu.make_async_copy(over.at[me], recvo.at[me], rsem.at[1, z]).start()

    sref[...] = stref[...].T
    s_half = sref[...].astype(BF16)
    for g in range(4):
        who, slot = place(iota((128, G), 1))
        spread = (who + PL * g == iota((128, G), 0)).astype(BF16)
        s_rep = jnp.dot(s_half, spread, preferred_element_type=F32)
        hot = (s_rep == slot.astype(F32)).astype(BF16)
        wmain[g] = hot[:, 0 : PL * MAIN]
        wovf[g] = hot[:, PL * MAIN : G]

    loads[0].wait()
    who, slot = place(iota((G, G), 0))
    perm = (CAP * who + slot == iota((G, G), 1)).astype(BF16)
    for q in range(2):
        for n in range(0, 2 * feat, 512):
            xin[q, :, n : n + 512] = jnp.dot(
                perm, sin[G * q : G * (q + 1), n : n + 512], preferred_element_type=F32
            ).astype(BF16)

    loads[1].wait()
    loads[2].wait()
    for c in weight_copies():
        c.wait()
    for n in range(0, wd.shape[1], 256):
        cols = slice(n, n + 256)

        def gated(q, carry):
            a, b = xin[q, :, 0:feat], xin[q, :, feat : 2 * feat]
            gate = jnp.dot(a, wg[0, :, cols], preferred_element_type=F32) + jnp.dot(
                b, wg[1, :, cols], preferred_element_type=F32
            )
            up = jnp.dot(a, wu[0, :, cols], preferred_element_type=F32) + jnp.dot(
                b, wu[1, :, cols], preferred_element_type=F32
            )
            sg = jax.nn.sigmoid(gate)
            silu = gate * sg
            cm[q, :, cols] = silu
            bm[q, :, cols] = up * sg * (1.0 + gate * (1.0 - sg))
            hid[f, q, :, cols] = (silu * up).astype(BF16)
            return carry

        lax.fori_loop(0, 2, gated, 0)

    hid_copy = pltpu.make_async_remote_copy(
        src_ref=hid.at[f], dst_ref=hid.at[f], send_sem=hsem.at[0], recv_sem=hsem.at[1],
        device_id=(me, 1 - f), device_id_type=MESH,
    )
    hid_copy.start()
    loads[3].wait()

    def arrived(refs, sems, g):
        for b, ref in enumerate(refs):
            slab = ref.at[pl.ds(PL * g, PL)]
            pltpu.make_async_copy(slab, slab, sems.at[b, g]).wait()

    def unpack(g):
        arrived((recv, recvo), rsem, g)
        xs[g, 0 : PL * MAIN, :] = recv[pl.ds(PL * g, PL)].reshape(PL * MAIN, feat)
        xs[g, PL * MAIN : G, :] = recvo[pl.ds(PL * g, PL)].reshape(PL * REST, feat)

    def partial_copy(q):
        return pltpu.make_async_remote_copy(
            src_ref=psend.at[q], dst_ref=precv.at[q], send_sem=psem.at[0, q], recv_sem=psem.at[1, q],
            device_id=(me, 1 - f), device_id_type=MESH,
        )

    def back(i, carry):
        q = (z + 1 + i) % 2
        unpack(2 * (1 - f) + q)
        psend[q] = jnp.dot(xs[2 * (1 - f) + q], wd[...], preferred_element_type=F32)
        partial_copy(q).start()
        unpack(2 * f + q)
        pown[...] = jnp.dot(xs[2 * f + q], wd[...], preferred_element_type=F32)
        partial_copy(q).wait_recv()
        raw = pown[...] + precv[q]
        gpg[...] = (raw * bm[q]).astype(BF16)
        upg[...] = (raw * cm[q]).astype(BF16)
        gates = jnp.sum(raw * hid[f, q].astype(F32), axis=1, keepdims=True)
        _, slot = place(iota((G, 128), 0))
        spread = jnp.where(iota((G, 128), 1) == slot, gates, 0.0).astype(BF16)
        who, _ = place(iota((PL * REST, G), 1))
        table = jnp.dot(
            (who == iota((PL * REST, G), 0) // REST).astype(BF16), spread, preferred_element_type=F32
        ).astype(BF16)
        for h in range(2):
            over2[q, h, :, :, feat : feat + 128] = table.reshape(PL, REST, 128)
            for n in range(0, feat, 256):
                rows = (
                    lax.dot_general(
                        gpg[...], wg[h, n : n + 256, :], (((1,), (1,)), ((), ())), preferred_element_type=F32
                    )
                    + lax.dot_general(
                        upg[...], wu[h, n : n + 256, :], (((1,), (1,)), ((), ())), preferred_element_type=F32
                    )
                ).astype(BF16)
                msg2[q, h, :, :, n : n + 256] = rows[0 : PL * MAIN].reshape(PL, MAIN, 256)
                over2[q, h, :, :, n : n + 256] = rows[PL * MAIN : G].reshape(PL, REST, 256)

            def send(j, carry):
                blk = near((2 * f + q) * PL + me % PL, f, 0, (j * 5) % PL)
                here = jnp.logical_and(blk == me, h == f)

                for b, (src, dst) in enumerate(((msg2, rec2), (over2, rec2o))):

                    @pl.when(here)
                    def _():
                        pltpu.make_async_copy(src.at[q, h, blk % PL], dst.at[me], rsem2.at[b, z]).start()

                    @pl.when(jnp.logical_not(here))
                    def _():
                        pltpu.make_async_remote_copy(
                            src_ref=src.at[q, h, blk % PL], dst_ref=dst.at[me], send_sem=ssem2.at[b, q, h],
                            recv_sem=rsem2.at[b, z], device_id=(blk, h), device_id_type=MESH,
                        ).start()

                return carry

            lax.fori_loop(0, PL, send, 0)
        return carry

    pl.semaphore_wait(met.at[1], 1)
    lax.fori_loop(0, 2, back, 0)

    hid_copy.wait()
    inner = hid.shape[3]

    def down(m, carry):
        at = pl.multiple_of(m * 256, 256)
        lhs = xs[:, :, pl.ds(at, 256)].reshape(4 * G, 256)
        dgv[0, pl.ds(at, 256), :] = lax.dot_general(
            lhs, hid[...].reshape(4 * G, inner), (((0,), (0,)), ((), ())), preferred_element_type=F32
        )
        return carry

    lax.fori_loop(0, feat // 256, down, 0)

    acc[...] = jnp.zeros_like(acc)

    def home(i, carry):
        g = (z + 1 + 2 * i - 3 * (i // 2)) % 4
        arrived((rec2, rec2o), rsem2, g)
        rest = rec2o[pl.ds(PL * g, PL)].reshape(PL * REST, feat + 128)
        gm[g] = rest[:, feat : feat + 128]
        acc[...] += jnp.dot(
            wmain[g], rec2[pl.ds(PL * g, PL)].reshape(PL * MAIN, feat), preferred_element_type=F32
        ) + jnp.dot(wovf[g], rest[:, 0:feat], preferred_element_type=F32)
        return carry

    lax.fori_loop(0, 4, home, 0)
    ig_ref[...] = acc[...].astype(BF16)

    table = gm[...].reshape(E * REST, 128)
    values = jnp.zeros((8, 128), F32)
    for k in range(top):
        hit = ids_ref[k : k + 1, :] == row
        slot = jnp.sum(jnp.where(hit, stref[...], 0.0), axis=0, keepdims=True)
        once = jnp.logical_and(ids_ref[k : k + 1, :] == row // REST, row % REST == 0)
        line = lax.dot_general(
            table, once.astype(BF16), (((0,), (0,)), ((), ())), preferred_element_type=F32
        )
        value = jnp.sum(jnp.where(row.astype(F32) == slot, line, 0.0), axis=0, keepdims=True)
        value = value / prob_ref[k : k + 1, :].astype(BF16).astype(F32)
        values = jnp.where(row[0:8] == k, value, values)
    gg_ref[...] = values[0:top].astype(BF16)

    for b, ref in enumerate((msg, over)):
        most = ref.at[pl.ds(0, E - 1)]
        pltpu.make_async_copy(most, most, ssem.at[b]).wait()
    for q in range(2):
        partial_copy(q).wait_send()
        for h in range(2):
            local = jnp.logical_and(z == 2 * f + q, f == h)

            for b, ref in enumerate((msg2, over2)):

                @pl.when(local)
                def _():
                    part = ref.at[q, h, pl.ds(0, PL - 1)]
                    pltpu.make_async_copy(part, part, ssem2.at[b, q, h]).wait()

                @pl.when(jnp.logical_not(local))
                def _():
                    pltpu.make_async_copy(ref.at[q, h], ref.at[q, h], ssem2.at[b, q, h]).wait()


def flush(ig_ref, gg_ref, dg_ref, ig_out, gg_out, dg_out, sems):
    parts = 4
    rows = dg_ref.shape[1] // parts
    copies = [
        pltpu.make_async_copy(dg_ref.at[0, pl.ds(rows * i, rows)], dg_out.at[0, pl.ds(rows * i, rows)], sems.at[i])
        for i in range(parts)
    ]
    copies.append(pltpu.make_async_copy(ig_ref, ig_out, sems.at[parts]))
    copies.append(pltpu.make_async_copy(gg_ref, gg_out, sems.at[parts + 1]))
    for c in copies:
        c.start()
    for c in copies:
        c.wait()


def body(out_grad, expert_ids, gate_probs, saved_inputs, gate_weight, up_weight, down_weight):
    tokens, feat = out_grad.shape
    top = expert_ids.shape[1]
    hidden = down_weight.shape[2]
    wide = feat + 128
    dma = pltpu.SemaphoreType.DMA
    vmem = pl.BlockSpec(memory_space=pltpu.VMEM)
    hbm = pl.BlockSpec(memory_space=pl.ANY)
    results = pl.pallas_call(
        kernel,
        out_shape=(
            pltpu.VMEM((tokens, feat), BF16),
            pltpu.VMEM((top, tokens), BF16),
            pltpu.VMEM((1, feat, hidden), F32),
        ),
        in_specs=[vmem, vmem, vmem, hbm, hbm, hbm, hbm],
        out_specs=(vmem, vmem, vmem),
        scratch_shapes=[
            pltpu.VMEM((E, MAIN, feat), BF16),
            pltpu.VMEM((E, REST, feat), BF16),
            pltpu.VMEM((E, MAIN, feat), BF16),
            pltpu.VMEM((E, REST, feat), BF16),
            pltpu.VMEM((4, G, feat), BF16),
            pltpu.VMEM((2 * G, 2 * feat), BF16),
            pltpu.VMEM((2, G, 2 * feat), BF16),
            pltpu.VMEM((2, feat, hidden), BF16),
            pltpu.VMEM((2, feat, hidden), BF16),
            pltpu.VMEM((feat, hidden), BF16),
            pltpu.VMEM((2, G, hidden), F32),
            pltpu.VMEM((2, G, hidden), F32),
            pltpu.VMEM((2, 2, G, hidden), BF16),
            pltpu.VMEM((G, hidden), F32),
            pltpu.VMEM((2, G, hidden), F32),
            pltpu.VMEM((2, G, hidden), F32),
            pltpu.VMEM((G, hidden), BF16),
            pltpu.VMEM((G, hidden), BF16),
            pltpu.VMEM((2, 2, PL, MAIN, feat), BF16),
            pltpu.VMEM((2, 2, PL, REST, wide), BF16),
            pltpu.VMEM((E, MAIN, feat), BF16),
            pltpu.VMEM((E, REST, wide), BF16),
            pltpu.VMEM((4, tokens, PL * MAIN), BF16),
            pltpu.VMEM((4, tokens, G - PL * MAIN), BF16),
            pltpu.VMEM((4, PL * REST, 128), BF16),
            pltpu.VMEM((tokens, feat), F32),
            pltpu.VMEM((tokens, 128), F32),
            pltpu.VMEM((128, tokens), F32),
            pltpu.VMEM((128, tokens), F32),
            dma((4,)),
            dma((2, 2)),
            dma((2,)),
            dma((2, 2)),
            dma((2,)),
            dma((2, 4)),
            dma((2, 2, 2)),
            dma((2, 4)),
            pltpu.SemaphoreType.REGULAR((2,)),
        ],
        compiler_params=pltpu.CompilerParams(
            collective_id=0, has_side_effects=True, vmem_limit_bytes=50 << 20
        ),
    )(expert_ids.T, gate_probs.T, out_grad, saved_inputs, gate_weight, up_weight, down_weight)
    input_grad, gate_grad, down_grad = pl.pallas_call(
        flush,
        out_shape=(
            pltpu.HBM((tokens, feat), BF16),
            pltpu.HBM((top, tokens), BF16),
            pltpu.HBM((1, feat, hidden), F32),
        ),
        in_specs=[vmem, vmem, vmem],
        out_specs=(hbm, hbm, hbm),
        scratch_shapes=[dma((6,))],
        compiler_params=pltpu.CompilerParams(vmem_limit_bytes=4 << 20),
    )(*[pltpu.with_memory_space_constraint(r, pltpu.VMEM) for r in results])
    return input_grad, gate_grad.T, down_grad


def solution(mesh):
    placed = (
        P("expert", "fsdp"),
        P("expert", None),
        P("expert", None),
        P("expert", "fsdp", None),
        P("expert", "fsdp", None),
        P("expert", "fsdp", None),
        P("expert", "fsdp", None),
    )
    return jax.shard_map(
        body,
        mesh=mesh,
        in_specs=placed,
        out_specs=(P("expert", "fsdp"), P("expert", None), P("expert", "fsdp", None)),
        check_vma=False,
    )
```

```python
import functools

import jax
import jax.numpy as jnp
from jax import lax
from jax.experimental import pallas as pl
from jax.experimental.pallas import tpu as pltpu
from jax.sharding import PartitionSpec as P

MESH = pl.DeviceIdType.MESH
F32 = jnp.float32
BF16 = jnp.bfloat16
E = 64
PL = 16
CAP = 18
MAIN = 16
REST = CAP - MAIN
G = PL * CAP


def iota(shape, dim):
    return lax.broadcasted_iota(jnp.int32, shape, dim)


def near(me, f, dz, yx):
    sign = 1 - 2 * f
    z = (me // 16 + 4 + sign * dz) % 4
    y = ((me // 4) % 4 + 4 + sign * (yx // 4)) % 4
    x = (me % 4 + 4 + sign * (yx % 4)) % 4
    return z * 16 + y * 4 + x


def kernel(
    ids_ref, prob_ref, og_ref, sin_hbm, gw_hbm, uw_hbm, dw_hbm,
    ig_ref, gg_ref, dgv,
    ag0, ag1, ag2, idp, idpg, lhs, msg0, msg1, msg2_, over0, over1, over2_,
    got0, got1, got2, goto0, goto1, goto2, xs, sin, xin, wg, wu, wd, bm, cm, hid, pown, psend, precv, gpg, upg,
    msg2, over2, rec2, rec2o, wmain, wovf, gm, acc, sref, stref,
    lsem, wsem, hsem, psem, ssem, rsem, ssem2, rsem2, asem, bsem,
):
    me = lax.axis_index("expert")
    f = lax.axis_index("fsdp")
    z = me // PL
    feat = og_ref.shape[1]
    top = ids_ref.shape[0]

    loads = [
        pltpu.make_async_copy(sin_hbm.at[0], sin, lsem.at[0]),
        pltpu.make_async_copy(gw_hbm.at[0], wg.at[f], lsem.at[1]),
        pltpu.make_async_copy(uw_hbm.at[0], wu.at[f], lsem.at[2]),
        pltpu.make_async_copy(dw_hbm.at[0], wd, lsem.at[3]),
    ]
    for c in loads:
        c.start()

    barrier = pltpu.get_barrier_semaphore()

    y, x = (me // 4) % 4, me % 4
    mine = (z, y, x)
    step_of = (PL, 4, 1)
    spans = ((0, 512), (512, 896), (896, 1280))
    gathered, sent, sent_over = (ag0, ag1, ag2), (msg0, msg1, msg2_), (over0, over1, over2_)
    got, got_over = (got0, got1, got2), (goto0, goto1, goto2)

    def mate(a, d):
        return me + (((mine[a] + d) % 4) - mine[a]) * step_of[a]

    for a in range(3):
        for d in (1, 2, 3):
            pl.semaphore_signal(barrier, inc=1, device_id=(mate(a, d), f), device_id_type=MESH)
    pl.semaphore_signal(barrier, inc=1, device_id=(me, 1 - f), device_id_type=MESH)

    idp[...] = jnp.zeros_like(idp)
    idp[0:top, :] = ids_ref[...].astype(F32)
    idp[8 : 8 + top, :] = prob_ref[...]
    for a, (lo, hi) in enumerate(spans):
        gathered[a][mine[a]] = og_ref[:, lo:hi]
        idpg[a, mine[a]] = idp[...]
    lane = iota((128, 128), 1)
    row = iota((128, 128), 0)
    before = (row < lane).astype(BF16)

    def line_copy(k, a, d):
        lo, hi = spans[a]
        src, dst = ((idp, idpg.at[a, mine[a]]), (og_ref.at[:, lo:hi], gathered[a].at[mine[a]]))[k]
        return pltpu.make_async_remote_copy(
            src_ref=src, dst_ref=dst, send_sem=asem.at[k, a], recv_sem=bsem.at[k, a],
            device_id=(mate(a, d), f), device_id_type=MESH,
        )

    pl.semaphore_wait(barrier, 10)
    for a in range(3):
        for d in (1, 3, 2):
            line_copy(0, a, d).start()
    for d in (2, 1, 3):
        for a in range(3):
            line_copy(1, a, d).start()

    def place(r):
        main = r < PL * MAIN
        rest = r - PL * MAIN
        return jnp.where(main, r // MAIN, rest // REST), jnp.where(main, r % MAIN, MAIN + rest % REST)

    def place_tokens(a, b):
        table = idpg[a, b]
        p = iota((PL, 128), 0)
        u, v = p // 4, p % 4
        expert = (PL * z + p, PL * u + 4 * y + v, PL * u + 4 * v + x)[a].astype(F32)
        names = jnp.zeros((PL, 128), F32)
        probs = jnp.zeros((PL, 128), F32)
        for k in range(top):
            hit = table[k : k + 1, :] == expert
            names = names + hit.astype(F32)
            probs = probs + jnp.where(hit, table[8 + k : 9 + k, :], 0.0)
        rank = jnp.dot(names.astype(BF16), before, preferred_element_type=F32)
        st = jnp.where(names > 0.0, rank, -1.0).astype(BF16)
        who, _ = place(iota((G, PL), 0))
        _, slot = place(iota((G, 128), 0))
        spread = (who == iota((G, PL), 1)).astype(BF16)
        s_rep = jnp.dot(spread, st, preferred_element_type=F32)
        p_rep = jnp.dot(spread, probs.astype(BF16), preferred_element_type=F32)
        lhs[a, b] = jnp.where(s_rep == slot.astype(F32), p_rep, 0.0).astype(BF16)

    def build(a, b):
        rows = jnp.dot(lhs[a, b], gathered[a][b], preferred_element_type=F32).astype(BF16)
        wide = rows.shape[1]
        main, rest = rows[0 : PL * MAIN], rows[PL * MAIN : G]
        if a == 0:
            sent[a][b % 2, :, b // 2] = main.reshape(PL, MAIN, wide)
            sent_over[a][b % 2, :, b // 2] = rest.reshape(PL, REST, wide)
        else:
            sent[a][:, :, b] = main.reshape(4, 4, MAIN, wide)
            sent_over[a][:, :, b] = rest.reshape(4, 4, REST, wide)

    sign = 1 - 2 * f

    def dispatch(phase):
        half = (z + 1 + phase) % 2

        def plane_send(i, yx):
            dy, dx = yx // 4, yx % 4
            p = ((y + 4 + sign * dy) % 4) * 4 + (x + 4 + sign * dx) % 4
            for k, (src, dst) in enumerate(((msg0, got0), (over0, goto0))):

                @pl.when(yx == 0)
                def _():
                    pltpu.make_async_copy(src.at[half, p], dst.at[half, me % PL], rsem.at[k, 0, phase]).start()

                @pl.when(yx != 0)
                def _():
                    pltpu.make_async_remote_copy(
                        src_ref=src.at[half, p], dst_ref=dst.at[half, me % PL], send_sem=ssem.at[k, 0, phase],
                        recv_sem=rsem.at[k, 0, phase], device_id=(z * PL + p, f), device_id_type=MESH,
                    ).start()

        def cross_send(i, a):
            dz, dw = 1 - phase + 2 * (i % 2), i // 2
            to_z = (z + 4 + sign * dz) % 4
            w = mine[3 - a]
            to_w = (w + 4 + sign * dw) % 4
            d = to_z * PL + (y * 4 + to_w if a == 1 else to_w * 4 + x)
            for k, (src, dst) in enumerate(((sent[a], got[a]), (sent_over[a], got_over[a]))):
                there = dst.at[z % 2, z // 2, w]

                def local():
                    pltpu.make_async_copy(src.at[to_z, to_w], there, rsem.at[k, a, phase]).start()

                def remote():
                    pltpu.make_async_remote_copy(
                        src_ref=src.at[to_z, to_w], dst_ref=there, send_sem=ssem.at[k, a, phase],
                        recv_sem=rsem.at[k, a, phase], device_id=(d, f), device_id_type=MESH,
                    ).start()

                if phase == 0:
                    remote()
                else:
                    pl.when(i == 0)(local)
                    pl.when(i != 0)(remote)

        def step(i, carry):
            plane_send(i, (10 * i) % PL)
            cross_send(i, 1)
            plane_send(i, (10 * i + 5) % PL)
            cross_send(i, 2)
            return carry

        lax.fori_loop(0, 8, step, 0)

    def weight_copies():
        return [
            pltpu.make_async_remote_copy(
                src_ref=h.at[0], dst_ref=w.at[f], send_sem=wsem.at[0, i], recv_sem=wsem.at[1, i],
                device_id=(me, 1 - f), device_id_type=MESH,
            )
            for i, (h, w) in enumerate(((gw_hbm, wg), (uw_hbm, wu)))
        ]

    for c in weight_copies():
        c.start()
    def line_wait(k, refs):
        for a, ref in enumerate(refs):
            three = ref.at[pl.ds(0, 3)]
            pltpu.make_async_copy(three, three, bsem.at[k, a]).wait()

    line_wait(0, [idpg.at[a] for a in range(3)])
    for a in range(3):
        for b in range(4):
            place_tokens(a, b)
    line_wait(1, gathered)
    for a in range(3):
        for b in range(4):
            build(a, b)
    dispatch(0)
    dispatch(1)

    names = jnp.zeros((128, 128), F32)
    for k in range(top):
        names = names + (ids_ref[k : k + 1, :] == row).astype(F32)
    rank = jnp.dot(names.astype(BF16), before, preferred_element_type=F32)
    stref[...] = jnp.where(names > 0.0, rank, -1.0)

    sref[...] = stref[...].T
    s_half = sref[...].astype(BF16)
    for g in range(4):
        who, slot = place(iota((128, G), 1))
        spread = (who + PL * g == iota((128, G), 0)).astype(BF16)
        s_rep = jnp.dot(s_half, spread, preferred_element_type=F32)
        hot = (s_rep == slot.astype(F32)).astype(BF16)
        wmain[g] = hot[:, 0 : PL * MAIN]
        wovf[g] = hot[:, PL * MAIN : G]

    loads[0].wait()
    who, slot = place(iota((G, G), 0))
    perm = (CAP * who + slot == iota((G, G), 1)).astype(BF16)
    for q in range(2):
        for n in range(0, 2 * feat, 512):
            xin[q, :, n : n + 512] = jnp.dot(
                perm, sin[G * q : G * (q + 1), n : n + 512], preferred_element_type=F32
            ).astype(BF16)

    loads[1].wait()
    loads[2].wait()
    for c in weight_copies():
        c.wait()
    for n in range(0, wd.shape[1], 256):
        cols = slice(n, n + 256)

        def gated(q, carry):
            a, b = xin[q, :, 0:feat], xin[q, :, feat : 2 * feat]
            gate = jnp.dot(a, wg[0, :, cols], preferred_element_type=F32) + jnp.dot(
                b, wg[1, :, cols], preferred_element_type=F32
            )
            up = jnp.dot(a, wu[0, :, cols], preferred_element_type=F32) + jnp.dot(
                b, wu[1, :, cols], preferred_element_type=F32
            )
            sg = jax.nn.sigmoid(gate)
            silu = gate * sg
            cm[q, :, cols] = silu
            bm[q, :, cols] = up * sg * (1.0 + gate * (1.0 - sg))
            hid[f, q, :, cols] = (silu * up).astype(BF16)
            return carry

        lax.fori_loop(0, 2, gated, 0)

    hid_copy = pltpu.make_async_remote_copy(
        src_ref=hid.at[f], dst_ref=hid.at[f], send_sem=hsem.at[0], recv_sem=hsem.at[1],
        device_id=(me, 1 - f), device_id_type=MESH,
    )
    hid_copy.start()
    loads[3].wait()

    def arrived(refs, sems, g):
        for b, ref in enumerate(refs):
            slab = ref.at[pl.ds(PL * g, PL)]
            pltpu.make_async_copy(slab, slab, sems.at[b, g]).wait()

    def wait_phase(phase, half):
        for a in range(3):
            for k, ref in enumerate((got[a], got_over[a])):
                pltpu.make_async_copy(ref.at[half], ref.at[half], rsem.at[k, a, phase]).wait()

    def unpack(half, top_half):
        g = 2 * top_half + half
        n = PL * MAIN
        for a, (lo, hi) in enumerate(spans):
            if a == 0:
                xs[g, 0:n, lo:hi] = got[a][half, :, top_half].reshape(n, hi - lo)
                xs[g, n:G, lo:hi] = got_over[a][half, :, top_half].reshape(G - n, hi - lo)
            elif a == 1:
                for b in range(4):
                    xs[g, 64 * b : 64 * b + 64, lo:hi] = got[a][half, top_half, :, b].reshape(64, hi - lo)
                rest = jnp.concatenate([got_over[a][half, top_half, :, b] for b in range(4)], axis=0)
                xs[g, n:G, lo:hi] = rest.reshape(G - n, hi - lo)
            else:
                xs[g, 0:n, lo:hi] = got[a][half, top_half].reshape(n, hi - lo)
                xs[g, n:G, lo:hi] = got_over[a][half, top_half].reshape(G - n, hi - lo)

    def partial_copy(q):
        return pltpu.make_async_remote_copy(
            src_ref=psend.at[q], dst_ref=precv.at[q], send_sem=psem.at[0, q], recv_sem=psem.at[1, q],
            device_id=(me, 1 - f), device_id_type=MESH,
        )

    def back(i, carry):
        q = (z + 1 + i) % 2
        wait_phase(i, q)
        unpack(q, 1 - f)
        psend[q] = jnp.dot(xs[2 * (1 - f) + q], wd[...], preferred_element_type=F32)
        partial_copy(q).start()
        unpack(q, f)
        pown[...] = jnp.dot(xs[2 * f + q], wd[...], preferred_element_type=F32)
        partial_copy(q).wait_recv()
        raw = pown[...] + precv[q]
        gpg[...] = (raw * bm[q]).astype(BF16)
        upg[...] = (raw * cm[q]).astype(BF16)
        gates = jnp.sum(raw * hid[f, q].astype(F32), axis=1, keepdims=True)
        _, slot = place(iota((G, 128), 0))
        spread = jnp.where(iota((G, 128), 1) == slot, gates, 0.0).astype(BF16)
        who, _ = place(iota((PL * REST, G), 1))
        table = jnp.dot(
            (who == iota((PL * REST, G), 0) // REST).astype(BF16), spread, preferred_element_type=F32
        ).astype(BF16)
        for h in range(2):
            over2[q, h, :, :, feat : feat + 128] = table.reshape(PL, REST, 128)
            for n in range(0, feat, 256):
                rows = (
                    lax.dot_general(
                        gpg[...], wg[h, n : n + 256, :], (((1,), (1,)), ((), ())), preferred_element_type=F32
                    )
                    + lax.dot_general(
                        upg[...], wu[h, n : n + 256, :], (((1,), (1,)), ((), ())), preferred_element_type=F32
                    )
                ).astype(BF16)
                msg2[q, h, :, :, n : n + 256] = rows[0 : PL * MAIN].reshape(PL, MAIN, 256)
                over2[q, h, :, :, n : n + 256] = rows[PL * MAIN : G].reshape(PL, REST, 256)

            def send(j, carry):
                blk = near((2 * f + q) * PL + me % PL, f, 0, (j * 7) % PL)
                here = jnp.logical_and(blk == me, h == f)

                for b, (src, dst) in enumerate(((msg2, rec2), (over2, rec2o))):

                    @pl.when(here)
                    def _():
                        pltpu.make_async_copy(src.at[q, h, blk % PL], dst.at[me], rsem2.at[b, z]).start()

                    @pl.when(jnp.logical_not(here))
                    def _():
                        pltpu.make_async_remote_copy(
                            src_ref=src.at[q, h, blk % PL], dst_ref=dst.at[me], send_sem=ssem2.at[b, q, h],
                            recv_sem=rsem2.at[b, z], device_id=(blk, h), device_id_type=MESH,
                        ).start()

                return carry

            lax.fori_loop(0, PL, send, 0)
        return carry

    lax.fori_loop(0, 2, back, 0)

    hid_copy.wait()
    inner = hid.shape[3]

    def down(m, carry):
        at = pl.multiple_of(m * 256, 256)
        lhs = xs[:, :, pl.ds(at, 256)].reshape(4 * G, 256)
        dgv[0, pl.ds(at, 256), :] = lax.dot_general(
            lhs, hid[...].reshape(4 * G, inner), (((0,), (0,)), ((), ())), preferred_element_type=F32
        )
        return carry

    lax.fori_loop(0, feat // 256, down, 0)

    acc[...] = jnp.zeros_like(acc)

    def home(i, carry):
        g = (z + 1 + 2 * i - 3 * (i // 2)) % 4
        arrived((rec2, rec2o), rsem2, g)
        rest = rec2o[pl.ds(PL * g, PL)].reshape(PL * REST, feat + 128)
        gm[g] = rest[:, feat : feat + 128]
        acc[...] += jnp.dot(
            wmain[g], rec2[pl.ds(PL * g, PL)].reshape(PL * MAIN, feat), preferred_element_type=F32
        ) + jnp.dot(wovf[g], rest[:, 0:feat], preferred_element_type=F32)
        return carry

    lax.fori_loop(0, 4, home, 0)
    ig_ref[...] = acc[...].astype(BF16)

    table = gm[...].reshape(E * REST, 128)
    values = jnp.zeros((8, 128), F32)
    for k in range(top):
        hit = ids_ref[k : k + 1, :] == row
        slot = jnp.sum(jnp.where(hit, stref[...], 0.0), axis=0, keepdims=True)
        once = jnp.logical_and(ids_ref[k : k + 1, :] == row // REST, row % REST == 0)
        line = lax.dot_general(
            table, once.astype(BF16), (((0,), (0,)), ((), ())), preferred_element_type=F32
        )
        value = jnp.sum(jnp.where(row.astype(F32) == slot, line, 0.0), axis=0, keepdims=True)
        value = value / prob_ref[k : k + 1, :].astype(BF16).astype(F32)
        values = jnp.where(row[0:8] == k, value, values)
    gg_ref[...] = values[0:top].astype(BF16)

    for a in range(3):
        for k, ref in enumerate((idpg.at[a], gathered[a])):
            three = ref.at[pl.ds(0, 3)]
            pltpu.make_async_copy(three, three, asem.at[k, a]).wait()
        for phase in range(2):
            for k, ref in enumerate((sent[a], sent_over[a])):
                if a == 0:
                    most = ref.at[0, pl.ds(0, PL - 1)]
                    pltpu.make_async_copy(most, most, ssem.at[k, a, phase]).wait()
                else:
                    for part in (ref.at[0], ref.at[1] if phase == 0 else ref.at[1, pl.ds(0, 3)]):
                        pltpu.make_async_copy(part, part, ssem.at[k, a, phase]).wait()
    for q in range(2):
        partial_copy(q).wait_send()
        for h in range(2):
            local = jnp.logical_and(z == 2 * f + q, f == h)

            for b, ref in enumerate((msg2, over2)):

                @pl.when(local)
                def _():
                    part = ref.at[q, h, pl.ds(0, PL - 1)]
                    pltpu.make_async_copy(part, part, ssem2.at[b, q, h]).wait()

                @pl.when(jnp.logical_not(local))
                def _():
                    pltpu.make_async_copy(ref.at[q, h], ref.at[q, h], ssem2.at[b, q, h]).wait()


def flush(ig_ref, gg_ref, dg_ref, ig_out, gg_out, dg_out, sems):
    parts = 4
    rows = dg_ref.shape[1] // parts
    copies = [
        pltpu.make_async_copy(dg_ref.at[0, pl.ds(rows * i, rows)], dg_out.at[0, pl.ds(rows * i, rows)], sems.at[i])
        for i in range(parts)
    ]
    copies.append(pltpu.make_async_copy(ig_ref, ig_out, sems.at[parts]))
    copies.append(pltpu.make_async_copy(gg_ref, gg_out, sems.at[parts + 1]))
    for c in copies:
        c.start()
    for c in copies:
        c.wait()


def body(out_grad, expert_ids, gate_probs, saved_inputs, gate_weight, up_weight, down_weight):
    tokens, feat = out_grad.shape
    top = expert_ids.shape[1]
    hidden = down_weight.shape[2]
    wide = feat + 128
    dma = pltpu.SemaphoreType.DMA
    vmem = pl.BlockSpec(memory_space=pltpu.VMEM)
    hbm = pl.BlockSpec(memory_space=pl.ANY)
    results = pl.pallas_call(
        kernel,
        out_shape=(
            pltpu.VMEM((tokens, feat), BF16),
            pltpu.VMEM((top, tokens), BF16),
            pltpu.VMEM((1, feat, hidden), F32),
        ),
        in_specs=[vmem, vmem, vmem, hbm, hbm, hbm, hbm],
        out_specs=(vmem, vmem, vmem),
        scratch_shapes=[
            pltpu.VMEM((4, tokens, 512), BF16),
            pltpu.VMEM((4, tokens, 384), BF16),
            pltpu.VMEM((4, tokens, 384), BF16),
            pltpu.VMEM((16, tokens), F32),
            pltpu.VMEM((3, 4, 16, tokens), F32),
            pltpu.VMEM((3, 4, G, tokens), BF16),
            pltpu.VMEM((2, PL, 2, MAIN, 512), BF16),
            pltpu.VMEM((4, 4, 4, MAIN, 384), BF16),
            pltpu.VMEM((4, 4, 4, MAIN, 384), BF16),
            pltpu.VMEM((2, PL, 2, REST, 512), BF16),
            pltpu.VMEM((4, 4, 4, REST, 384), BF16),
            pltpu.VMEM((4, 4, 4, REST, 384), BF16),
            pltpu.VMEM((2, PL, 2, MAIN, 512), BF16),
            pltpu.VMEM((2, 2, 4, 4, MAIN, 384), BF16),
            pltpu.VMEM((2, 2, 4, 4, MAIN, 384), BF16),
            pltpu.VMEM((2, PL, 2, REST, 512), BF16),
            pltpu.VMEM((2, 2, 4, 4, REST, 384), BF16),
            pltpu.VMEM((2, 2, 4, 4, REST, 384), BF16),
            pltpu.VMEM((4, G, feat), BF16),
            pltpu.VMEM((2 * G, 2 * feat), BF16),
            pltpu.VMEM((2, G, 2 * feat), BF16),
            pltpu.VMEM((2, feat, hidden), BF16),
            pltpu.VMEM((2, feat, hidden), BF16),
            pltpu.VMEM((feat, hidden), BF16),
            pltpu.VMEM((2, G, hidden), F32),
            pltpu.VMEM((2, G, hidden), F32),
            pltpu.VMEM((2, 2, G, hidden), BF16),
            pltpu.VMEM((G, hidden), F32),
            pltpu.VMEM((2, G, hidden), F32),
            pltpu.VMEM((2, G, hidden), F32),
            pltpu.VMEM((G, hidden), BF16),
            pltpu.VMEM((G, hidden), BF16),
            pltpu.VMEM((2, 2, PL, MAIN, feat), BF16),
            pltpu.VMEM((2, 2, PL, REST, wide), BF16),
            pltpu.VMEM((E, MAIN, feat), BF16),
            pltpu.VMEM((E, REST, wide), BF16),
            pltpu.VMEM((4, tokens, PL * MAIN), BF16),
            pltpu.VMEM((4, tokens, G - PL * MAIN), BF16),
            pltpu.VMEM((4, PL * REST, 128), BF16),
            pltpu.VMEM((tokens, feat), F32),
            pltpu.VMEM((tokens, 128), F32),
            pltpu.VMEM((128, tokens), F32),
            dma((4,)),
            dma((2, 2)),
            dma((2,)),
            dma((2, 2)),
            dma((2, 3, 2)),
            dma((2, 3, 2)),
            dma((2, 2, 2)),
            dma((2, 4)),
            dma((2, 3)),
            dma((2, 3)),
        ],
        compiler_params=pltpu.CompilerParams(
            collective_id=0, has_side_effects=True, vmem_limit_bytes=50 << 20
        ),
    )(expert_ids.T, gate_probs.T, out_grad, saved_inputs, gate_weight, up_weight, down_weight)
    input_grad, gate_grad, down_grad = pl.pallas_call(
        flush,
        out_shape=(
            pltpu.HBM((tokens, feat), BF16),
            pltpu.HBM((top, tokens), BF16),
            pltpu.HBM((1, feat, hidden), F32),
        ),
        in_specs=[vmem, vmem, vmem],
        out_specs=(hbm, hbm, hbm),
        scratch_shapes=[dma((6,))],
        compiler_params=pltpu.CompilerParams(vmem_limit_bytes=4 << 20),
    )(*[pltpu.with_memory_space_constraint(r, pltpu.VMEM) for r in results])
    return input_grad, gate_grad.T, down_grad


def solution(mesh):
    placed = (
        P("expert", "fsdp"),
        P("expert", None),
        P("expert", None),
        P("expert", "fsdp", None),
        P("expert", "fsdp", None),
        P("expert", "fsdp", None),
        P("expert", "fsdp", None),
    )
    return jax.shard_map(
        body,
        mesh=mesh,
        in_specs=placed,
        out_specs=(P("expert", "fsdp"), P("expert", None), P("expert", "fsdp", None)),
        check_vma=False,
    )
```

```python
import functools

import jax
import jax.numpy as jnp
from jax import lax
from jax.experimental import pallas as pl
from jax.experimental.pallas import tpu as pltpu
from jax.sharding import PartitionSpec as P

MESH = pl.DeviceIdType.MESH
F32 = jnp.float32
BF16 = jnp.bfloat16
E = 64
PL = 16
CAP = 18
MAIN = 16
REST = CAP - MAIN
G = PL * CAP


def iota(shape, dim):
    return lax.broadcasted_iota(jnp.int32, shape, dim)


def near(me, f, dz, yx):
    sign = 1 - 2 * f
    z = (me // 16 + 4 + sign * dz) % 4
    y = ((me // 4) % 4 + 4 + sign * (yx // 4)) % 4
    x = (me % 4 + 4 + sign * (yx % 4)) % 4
    return z * 16 + y * 4 + x


def kernel(
    ids_ref, prob_ref, og_ref, sin_hbm, gw_hbm, uw_hbm, dw_hbm,
    ig_ref, gg_ref, dgv,
    ag0, ag1, ag2, idp, idpg, lhs, msg0, msg1, msg2_, over0, over1, over2_,
    got0, got1, got2, goto0, goto1, goto2, xs, sin, xin, wg, wu, wd, bm, cm, hid, pown, psend, precv, gpg, upg,
    msg2, over2, rec2, rec2o, wmain, wovf, gm, acc, sref, stref,
    lsem, wsem, hsem, psem, ssem, rsem, ssem2, rsem2, asem, bsem,
):
    me = lax.axis_index("expert")
    f = lax.axis_index("fsdp")
    z = me // PL
    feat = og_ref.shape[1]
    top = ids_ref.shape[0]

    loads = [
        pltpu.make_async_copy(sin_hbm.at[0], sin, lsem.at[0]),
        pltpu.make_async_copy(gw_hbm.at[0], wg.at[f], lsem.at[1]),
        pltpu.make_async_copy(uw_hbm.at[0], wu.at[f], lsem.at[2]),
        pltpu.make_async_copy(dw_hbm.at[0], wd, lsem.at[3]),
    ]
    for c in loads:
        c.start()

    barrier = pltpu.get_barrier_semaphore()

    y, x = (me // 4) % 4, me % 4
    mine = (z, y, x)
    step_of = (PL, 4, 1)
    spans = ((0, 512), (512, 896), (896, 1280))
    gathered, sent, sent_over = (ag0, ag1, ag2), (msg0, msg1, msg2_), (over0, over1, over2_)
    got, got_over = (got0, got1, got2), (goto0, goto1, goto2)

    def mate(a, d):
        return me + (((mine[a] + d) % 4) - mine[a]) * step_of[a]

    for a in range(3):
        for d in (1, 2, 3):
            pl.semaphore_signal(barrier, inc=1, device_id=(mate(a, d), f), device_id_type=MESH)
    pl.semaphore_signal(barrier, inc=1, device_id=(me, 1 - f), device_id_type=MESH)

    idp[...] = jnp.zeros_like(idp)
    idp[0:top, :] = ids_ref[...].astype(F32)
    idp[8 : 8 + top, :] = prob_ref[...]
    for a, (lo, hi) in enumerate(spans):
        gathered[a][mine[a]] = og_ref[:, lo:hi]
        idpg[a, mine[a]] = idp[...]
    lane = iota((128, 128), 1)
    row = iota((128, 128), 0)
    before = (row < lane).astype(BF16)

    def line_copy(k, a, d):
        lo, hi = spans[a]
        src, dst = ((idp, idpg.at[a, mine[a]]), (og_ref.at[:, lo:hi], gathered[a].at[mine[a]]))[k]
        return pltpu.make_async_remote_copy(
            src_ref=src, dst_ref=dst, send_sem=asem.at[k, a], recv_sem=bsem.at[k, a],
            device_id=(mate(a, d), f), device_id_type=MESH,
        )

    pl.semaphore_wait(barrier, 10)
    for a in range(3):
        for d in (1, 3, 2):
            line_copy(0, a, d).start()
    for d in (2, 1, 3):
        for a in range(3):
            line_copy(1, a, d).start()

    def place(r):
        main = r < PL * MAIN
        rest = r - PL * MAIN
        return jnp.where(main, r // MAIN, rest // REST), jnp.where(main, r % MAIN, MAIN + rest % REST)

    def place_tokens(a, b):
        table = idpg[a, b]
        p = iota((PL, 128), 0)
        u, v = p // 4, p % 4
        expert = (PL * z + p, PL * u + 4 * y + v, PL * u + 4 * v + x)[a].astype(F32)
        names = jnp.zeros((PL, 128), F32)
        probs = jnp.zeros((PL, 128), F32)
        for k in range(top):
            hit = table[k : k + 1, :] == expert
            names = names + hit.astype(F32)
            probs = probs + jnp.where(hit, table[8 + k : 9 + k, :], 0.0)
        rank = jnp.dot(names.astype(BF16), before, preferred_element_type=F32)
        st = jnp.where(names > 0.0, rank, -1.0).astype(BF16)
        who, _ = place(iota((G, PL), 0))
        _, slot = place(iota((G, 128), 0))
        spread = (who == iota((G, PL), 1)).astype(BF16)
        s_rep = jnp.dot(spread, st, preferred_element_type=F32)
        p_rep = jnp.dot(spread, probs.astype(BF16), preferred_element_type=F32)
        lhs[a, b] = jnp.where(s_rep == slot.astype(F32), p_rep, 0.0).astype(BF16)

    def build(a, b):
        rows = jnp.dot(lhs[a, b], gathered[a][b], preferred_element_type=F32).astype(BF16)
        wide = rows.shape[1]
        main, rest = rows[0 : PL * MAIN], rows[PL * MAIN : G]
        if a == 0:
            sent[a][b % 2, :, b // 2] = main.reshape(PL, MAIN, wide)
            sent_over[a][b % 2, :, b // 2] = rest.reshape(PL, REST, wide)
        else:
            sent[a][:, :, b] = main.reshape(4, 4, MAIN, wide)
            sent_over[a][:, :, b] = rest.reshape(4, 4, REST, wide)

    sign = 1 - 2 * f

    def dispatch(phase):
        half = (z + 1 + phase) % 2

        def plane_send(i, yx):
            dy, dx = yx // 4, yx % 4
            p = ((y + 4 + sign * dy) % 4) * 4 + (x + 4 + sign * dx) % 4
            for k, (src, dst) in enumerate(((msg0, got0), (over0, goto0))):

                @pl.when(yx == 0)
                def _():
                    pltpu.make_async_copy(src.at[half, p], dst.at[half, me % PL], rsem.at[k, 0, phase]).start()

                @pl.when(yx != 0)
                def _():
                    pltpu.make_async_remote_copy(
                        src_ref=src.at[half, p], dst_ref=dst.at[half, me % PL], send_sem=ssem.at[k, 0, phase],
                        recv_sem=rsem.at[k, 0, phase], device_id=(z * PL + p, f), device_id_type=MESH,
                    ).start()

        def cross_send(i, a):
            dz, dw = 1 - phase + 2 * (i % 2), i // 2
            to_z = (z + 4 + sign * dz) % 4
            w = mine[3 - a]
            to_w = (w + 4 + sign * dw) % 4
            d = to_z * PL + (y * 4 + to_w if a == 1 else to_w * 4 + x)
            for k, (src, dst) in enumerate(((sent[a], got[a]), (sent_over[a], got_over[a]))):
                there = dst.at[z % 2, z // 2, w]

                def local():
                    pltpu.make_async_copy(src.at[to_z, to_w], there, rsem.at[k, a, phase]).start()

                def remote():
                    pltpu.make_async_remote_copy(
                        src_ref=src.at[to_z, to_w], dst_ref=there, send_sem=ssem.at[k, a, phase],
                        recv_sem=rsem.at[k, a, phase], device_id=(d, f), device_id_type=MESH,
                    ).start()

                if phase == 0:
                    remote()
                else:
                    pl.when(i == 0)(local)
                    pl.when(i != 0)(remote)

        def step(i, carry):
            plane_send(i, (10 * i) % PL)
            cross_send(i, 1)
            plane_send(i, (10 * i + 5) % PL)
            cross_send(i, 2)
            return carry

        lax.fori_loop(0, 8, step, 0)

    def weight_copies():
        return [
            pltpu.make_async_remote_copy(
                src_ref=h.at[0], dst_ref=w.at[f], send_sem=wsem.at[0, i], recv_sem=wsem.at[1, i],
                device_id=(me, 1 - f), device_id_type=MESH,
            )
            for i, (h, w) in enumerate(((gw_hbm, wg), (uw_hbm, wu)))
        ]

    for c in weight_copies():
        c.start()
    def line_wait(k, refs):
        for a, ref in enumerate(refs):
            three = ref.at[pl.ds(0, 3)]
            pltpu.make_async_copy(three, three, bsem.at[k, a]).wait()

    line_wait(0, [idpg.at[a] for a in range(3)])
    for a in range(3):
        for b in range(4):
            place_tokens(a, b)
    line_wait(1, gathered)
    for a in (1, 2):
        for b in range(4):
            build(a, b)
    for t in range(2):
        build(0, 2 * t + (z + 1) % 2)
    dispatch(0)
    for t in range(2):
        build(0, 2 * t + z % 2)
    dispatch(1)

    names = jnp.zeros((128, 128), F32)
    for k in range(top):
        names = names + (ids_ref[k : k + 1, :] == row).astype(F32)
    rank = jnp.dot(names.astype(BF16), before, preferred_element_type=F32)
    stref[...] = jnp.where(names > 0.0, rank, -1.0)

    sref[...] = stref[...].T
    s_half = sref[...].astype(BF16)
    for g in range(4):
        who, slot = place(iota((128, G), 1))
        spread = (who + PL * g == iota((128, G), 0)).astype(BF16)
        s_rep = jnp.dot(s_half, spread, preferred_element_type=F32)
        hot = (s_rep == slot.astype(F32)).astype(BF16)
        wmain[g] = hot[:, 0 : PL * MAIN]
        wovf[g] = hot[:, PL * MAIN : G]

    loads[0].wait()
    who, slot = place(iota((G, G), 0))
    perm = (CAP * who + slot == iota((G, G), 1)).astype(BF16)
    for q in range(2):
        for n in range(0, 2 * feat, 512):
            xin[q, :, n : n + 512] = jnp.dot(
                perm, sin[G * q : G * (q + 1), n : n + 512], preferred_element_type=F32
            ).astype(BF16)

    loads[1].wait()
    loads[2].wait()
    for c in weight_copies():
        c.wait()
    for n in range(0, wd.shape[1], 256):
        cols = slice(n, n + 256)

        def gated(q, carry):
            a, b = xin[q, :, 0:feat], xin[q, :, feat : 2 * feat]
            gate = jnp.dot(a, wg[0, :, cols], preferred_element_type=F32) + jnp.dot(
                b, wg[1, :, cols], preferred_element_type=F32
            )
            up = jnp.dot(a, wu[0, :, cols], preferred_element_type=F32) + jnp.dot(
                b, wu[1, :, cols], preferred_element_type=F32
            )
            sg = jax.nn.sigmoid(gate)
            silu = gate * sg
            cm[q, :, cols] = silu
            bm[q, :, cols] = up * sg * (1.0 + gate * (1.0 - sg))
            hid[f, q, :, cols] = (silu * up).astype(BF16)
            return carry

        lax.fori_loop(0, 2, gated, 0)

    hid_copy = pltpu.make_async_remote_copy(
        src_ref=hid.at[f], dst_ref=hid.at[f], send_sem=hsem.at[0], recv_sem=hsem.at[1],
        device_id=(me, 1 - f), device_id_type=MESH,
    )
    hid_copy.start()
    loads[3].wait()

    def arrived(refs, sems, g):
        for b, ref in enumerate(refs):
            slab = ref.at[pl.ds(PL * g, PL)]
            pltpu.make_async_copy(slab, slab, sems.at[b, g]).wait()

    def wait_phase(phase, half):
        for a in range(3):
            for k, ref in enumerate((got[a], got_over[a])):
                pltpu.make_async_copy(ref.at[half], ref.at[half], rsem.at[k, a, phase]).wait()

    def unpack(half, top_half):
        g = 2 * top_half + half
        n = PL * MAIN
        for a, (lo, hi) in enumerate(spans):
            if a == 0:
                xs[g, 0:n, lo:hi] = got[a][half, :, top_half].reshape(n, hi - lo)
                xs[g, n:G, lo:hi] = got_over[a][half, :, top_half].reshape(G - n, hi - lo)
            elif a == 1:
                for b in range(4):
                    xs[g, 64 * b : 64 * b + 64, lo:hi] = got[a][half, top_half, :, b].reshape(64, hi - lo)
                rest = jnp.concatenate([got_over[a][half, top_half, :, b] for b in range(4)], axis=0)
                xs[g, n:G, lo:hi] = rest.reshape(G - n, hi - lo)
            else:
                xs[g, 0:n, lo:hi] = got[a][half, top_half].reshape(n, hi - lo)
                xs[g, n:G, lo:hi] = got_over[a][half, top_half].reshape(G - n, hi - lo)

    def partial_copy(q):
        return pltpu.make_async_remote_copy(
            src_ref=psend.at[q], dst_ref=precv.at[q], send_sem=psem.at[0, q], recv_sem=psem.at[1, q],
            device_id=(me, 1 - f), device_id_type=MESH,
        )

    def back(i, carry):
        q = (z + 1 + i) % 2
        wait_phase(i, q)
        unpack(q, 1 - f)
        psend[q] = jnp.dot(xs[2 * (1 - f) + q], wd[...], preferred_element_type=F32)
        partial_copy(q).start()
        unpack(q, f)
        pown[...] = jnp.dot(xs[2 * f + q], wd[...], preferred_element_type=F32)
        partial_copy(q).wait_recv()
        raw = pown[...] + precv[q]
        gpg[...] = (raw * bm[q]).astype(BF16)
        upg[...] = (raw * cm[q]).astype(BF16)
        gates = jnp.sum(raw * hid[f, q].astype(F32), axis=1, keepdims=True)
        _, slot = place(iota((G, 128), 0))
        spread = jnp.where(iota((G, 128), 1) == slot, gates, 0.0).astype(BF16)
        who, _ = place(iota((PL * REST, G), 1))
        table = jnp.dot(
            (who == iota((PL * REST, G), 0) // REST).astype(BF16), spread, preferred_element_type=F32
        ).astype(BF16)
        for h in range(2):
            over2[q, h, :, :, feat : feat + 128] = table.reshape(PL, REST, 128)
            for n in range(0, feat, 256):
                rows = (
                    lax.dot_general(
                        gpg[...], wg[h, n : n + 256, :], (((1,), (1,)), ((), ())), preferred_element_type=F32
                    )
                    + lax.dot_general(
                        upg[...], wu[h, n : n + 256, :], (((1,), (1,)), ((), ())), preferred_element_type=F32
                    )
                ).astype(BF16)
                msg2[q, h, :, :, n : n + 256] = rows[0 : PL * MAIN].reshape(PL, MAIN, 256)
                over2[q, h, :, :, n : n + 256] = rows[PL * MAIN : G].reshape(PL, REST, 256)

            def send(j, carry):
                blk = near((2 * f + q) * PL + me % PL, f, 0, (j * 7) % PL)
                here = jnp.logical_and(blk == me, h == f)

                for b, (src, dst) in enumerate(((msg2, rec2), (over2, rec2o))):

                    @pl.when(here)
                    def _():
                        pltpu.make_async_copy(src.at[q, h, blk % PL], dst.at[me], rsem2.at[b, z]).start()

                    @pl.when(jnp.logical_not(here))
                    def _():
                        pltpu.make_async_remote_copy(
                            src_ref=src.at[q, h, blk % PL], dst_ref=dst.at[me], send_sem=ssem2.at[b, q, h],
                            recv_sem=rsem2.at[b, z], device_id=(blk, h), device_id_type=MESH,
                        ).start()

                return carry

            lax.fori_loop(0, PL, send, 0)
        return carry

    lax.fori_loop(0, 2, back, 0)

    hid_copy.wait()
    inner = hid.shape[3]

    def down(m, carry):
        at = pl.multiple_of(m * 256, 256)
        lhs = xs[:, :, pl.ds(at, 256)].reshape(4 * G, 256)
        dgv[0, pl.ds(at, 256), :] = lax.dot_general(
            lhs, hid[...].reshape(4 * G, inner), (((0,), (0,)), ((), ())), preferred_element_type=F32
        )
        return carry

    lax.fori_loop(0, feat // 256, down, 0)

    acc[...] = jnp.zeros_like(acc)

    def home(i, carry):
        g = (z + 1 + 2 * i - 3 * (i // 2)) % 4
        arrived((rec2, rec2o), rsem2, g)
        rest = rec2o[pl.ds(PL * g, PL)].reshape(PL * REST, feat + 128)
        gm[g] = rest[:, feat : feat + 128]
        acc[...] += jnp.dot(
            wmain[g], rec2[pl.ds(PL * g, PL)].reshape(PL * MAIN, feat), preferred_element_type=F32
        ) + jnp.dot(wovf[g], rest[:, 0:feat], preferred_element_type=F32)
        return carry

    lax.fori_loop(0, 4, home, 0)
    ig_ref[...] = acc[...].astype(BF16)

    table = gm[...].reshape(E * REST, 128)
    values = jnp.zeros((8, 128), F32)
    for k in range(top):
        hit = ids_ref[k : k + 1, :] == row
        slot = jnp.sum(jnp.where(hit, stref[...], 0.0), axis=0, keepdims=True)
        once = jnp.logical_and(ids_ref[k : k + 1, :] == row // REST, row % REST == 0)
        line = lax.dot_general(
            table, once.astype(BF16), (((0,), (0,)), ((), ())), preferred_element_type=F32
        )
        value = jnp.sum(jnp.where(row.astype(F32) == slot, line, 0.0), axis=0, keepdims=True)
        value = value / prob_ref[k : k + 1, :].astype(BF16).astype(F32)
        values = jnp.where(row[0:8] == k, value, values)
    gg_ref[...] = values[0:top].astype(BF16)

    for a in range(3):
        for k, ref in enumerate((idpg.at[a], gathered[a])):
            three = ref.at[pl.ds(0, 3)]
            pltpu.make_async_copy(three, three, asem.at[k, a]).wait()
        for phase in range(2):
            for k, ref in enumerate((sent[a], sent_over[a])):
                if a == 0:
                    most = ref.at[0, pl.ds(0, PL - 1)]
                    pltpu.make_async_copy(most, most, ssem.at[k, a, phase]).wait()
                else:
                    for part in (ref.at[0], ref.at[1] if phase == 0 else ref.at[1, pl.ds(0, 3)]):
                        pltpu.make_async_copy(part, part, ssem.at[k, a, phase]).wait()
    for q in range(2):
        partial_copy(q).wait_send()
        for h in range(2):
            local = jnp.logical_and(z == 2 * f + q, f == h)

            for b, ref in enumerate((msg2, over2)):

                @pl.when(local)
                def _():
                    part = ref.at[q, h, pl.ds(0, PL - 1)]
                    pltpu.make_async_copy(part, part, ssem2.at[b, q, h]).wait()

                @pl.when(jnp.logical_not(local))
                def _():
                    pltpu.make_async_copy(ref.at[q, h], ref.at[q, h], ssem2.at[b, q, h]).wait()


def flush(ig_ref, gg_ref, dg_ref, ig_out, gg_out, dg_out, sems):
    parts = 4
    rows = dg_ref.shape[1] // parts
    copies = [
        pltpu.make_async_copy(dg_ref.at[0, pl.ds(rows * i, rows)], dg_out.at[0, pl.ds(rows * i, rows)], sems.at[i])
        for i in range(parts)
    ]
    copies.append(pltpu.make_async_copy(ig_ref, ig_out, sems.at[parts]))
    copies.append(pltpu.make_async_copy(gg_ref, gg_out, sems.at[parts + 1]))
    for c in copies:
        c.start()
    for c in copies:
        c.wait()


def body(out_grad, expert_ids, gate_probs, saved_inputs, gate_weight, up_weight, down_weight):
    tokens, feat = out_grad.shape
    top = expert_ids.shape[1]
    hidden = down_weight.shape[2]
    wide = feat + 128
    dma = pltpu.SemaphoreType.DMA
    vmem = pl.BlockSpec(memory_space=pltpu.VMEM)
    hbm = pl.BlockSpec(memory_space=pl.ANY)
    results = pl.pallas_call(
        kernel,
        out_shape=(
            pltpu.VMEM((tokens, feat), BF16),
            pltpu.VMEM((top, tokens), BF16),
            pltpu.VMEM((1, feat, hidden), F32),
        ),
        in_specs=[vmem, vmem, vmem, hbm, hbm, hbm, hbm],
        out_specs=(vmem, vmem, vmem),
        scratch_shapes=[
            pltpu.VMEM((4, tokens, 512), BF16),
            pltpu.VMEM((4, tokens, 384), BF16),
            pltpu.VMEM((4, tokens, 384), BF16),
            pltpu.VMEM((16, tokens), F32),
            pltpu.VMEM((3, 4, 16, tokens), F32),
            pltpu.VMEM((3, 4, G, tokens), BF16),
            pltpu.VMEM((2, PL, 2, MAIN, 512), BF16),
            pltpu.VMEM((4, 4, 4, MAIN, 384), BF16),
            pltpu.VMEM((4, 4, 4, MAIN, 384), BF16),
            pltpu.VMEM((2, PL, 2, REST, 512), BF16),
            pltpu.VMEM((4, 4, 4, REST, 384), BF16),
            pltpu.VMEM((4, 4, 4, REST, 384), BF16),
            pltpu.VMEM((2, PL, 2, MAIN, 512), BF16),
            pltpu.VMEM((2, 2, 4, 4, MAIN, 384), BF16),
            pltpu.VMEM((2, 2, 4, 4, MAIN, 384), BF16),
            pltpu.VMEM((2, PL, 2, REST, 512), BF16),
            pltpu.VMEM((2, 2, 4, 4, REST, 384), BF16),
            pltpu.VMEM((2, 2, 4, 4, REST, 384), BF16),
            pltpu.VMEM((4, G, feat), BF16),
            pltpu.VMEM((2 * G, 2 * feat), BF16),
            pltpu.VMEM((2, G, 2 * feat), BF16),
            pltpu.VMEM((2, feat, hidden), BF16),
            pltpu.VMEM((2, feat, hidden), BF16),
            pltpu.VMEM((feat, hidden), BF16),
            pltpu.VMEM((2, G, hidden), F32),
            pltpu.VMEM((2, G, hidden), F32),
            pltpu.VMEM((2, 2, G, hidden), BF16),
            pltpu.VMEM((G, hidden), F32),
            pltpu.VMEM((2, G, hidden), F32),
            pltpu.VMEM((2, G, hidden), F32),
            pltpu.VMEM((G, hidden), BF16),
            pltpu.VMEM((G, hidden), BF16),
            pltpu.VMEM((2, 2, PL, MAIN, feat), BF16),
            pltpu.VMEM((2, 2, PL, REST, wide), BF16),
            pltpu.VMEM((E, MAIN, feat), BF16),
            pltpu.VMEM((E, REST, wide), BF16),
            pltpu.VMEM((4, tokens, PL * MAIN), BF16),
            pltpu.VMEM((4, tokens, G - PL * MAIN), BF16),
            pltpu.VMEM((4, PL * REST, 128), BF16),
            pltpu.VMEM((tokens, feat), F32),
            pltpu.VMEM((tokens, 128), F32),
            pltpu.VMEM((128, tokens), F32),
            dma((4,)),
            dma((2, 2)),
            dma((2,)),
            dma((2, 2)),
            dma((2, 3, 2)),
            dma((2, 3, 2)),
            dma((2, 2, 2)),
            dma((2, 4)),
            dma((2, 3)),
            dma((2, 3)),
        ],
        compiler_params=pltpu.CompilerParams(
            collective_id=0, has_side_effects=True, vmem_limit_bytes=50 << 20
        ),
    )(expert_ids.T, gate_probs.T, out_grad, saved_inputs, gate_weight, up_weight, down_weight)
    input_grad, gate_grad, down_grad = pl.pallas_call(
        flush,
        out_shape=(
            pltpu.HBM((tokens, feat), BF16),
            pltpu.HBM((top, tokens), BF16),
            pltpu.HBM((1, feat, hidden), F32),
        ),
        in_specs=[vmem, vmem, vmem],
        out_specs=(hbm, hbm, hbm),
        scratch_shapes=[dma((6,))],
        compiler_params=pltpu.CompilerParams(vmem_limit_bytes=4 << 20),
    )(*[pltpu.with_memory_space_constraint(r, pltpu.VMEM) for r in results])
    return input_grad, gate_grad.T, down_grad


def solution(mesh):
    placed = (
        P("expert", "fsdp"),
        P("expert", None),
        P("expert", None),
        P("expert", "fsdp", None),
        P("expert", "fsdp", None),
        P("expert", "fsdp", None),
        P("expert", "fsdp", None),
    )
    return jax.shard_map(
        body,
        mesh=mesh,
        in_specs=placed,
        out_specs=(P("expert", "fsdp"), P("expert", None), P("expert", "fsdp", None)),
        check_vma=False,
    )
```
